32 devices in a mesh: groups: 2 (over y), grow: 4 (over z), cross: 2 (over x), side: 2 (over core).
Axes of the slice: x: 2, y: 2, z: 4, core: 2. Of those that a mesh axis runs over, the one named last changes fastest.
Arguments:
- phase_field: float32 [32, 64, 1024], P(('groups', 'grow'), 'cross', 'side'), parts along dimension 0, may hold values from -1.1 to 1.1
- solute_field: float32 [32, 64, 1024], P(('groups', 'grow'), 'cross', 'side'), parts along dimension 0, may hold values from -1 to 0.2
- shift_step: int32 [2], P('groups'), parts along dimension 0, may hold values from 0 to 1
- inflow_seed: int32 [128, 1024], P(('groups', 'cross'), 'side'), parts along dimension 0, may hold values from 0 to 1023
Outputs:
- phase_out: float32 [32, 64, 1024], P(('groups', 'grow'), 'cross', 'side'), parts along dimension 0
- solute_out: float32 [32, 64, 1024], P(('groups', 'grow'), 'cross', 'side'), parts along dimension 0
The draws below stay inside these ranges and needn't reach their ends.
There are 2 independent parts, one for each index of `groups`. The reference program is written for one: setup_inputs(seed, part) draws one part's arguments, and reference() takes and returns one part's arrays. A program takes and returns all parts, laid end to end along the dimension named above; each array names one. Nothing has to cross between parts.
Inputs may be any that keep to these rules, and one draw needn't show every extreme that they name: `shift_step`: the frame moves once, between two of the 3 steps.
All inputs are finite; a program needn't handle non-finite values.
Results may differ from the reference program's by a relative error of at most 0.00002.
Values sent between devices are 32-bit elements; how exact they have to be, the bound alone decides.
No kernel may reach another device: no remote copies, remote signals or barrier semaphores. Data moves between devices by JAX's collectives and lax.ppermute only.
A program may use at most 64 MiB of HBM per device.

```python
import jax
import jax.numpy as jnp

ITERS = 3
NZ = 16
NY = 64
NX = 1024


def set_ends(entries, own_key, smallest, largest):
    extent = entries.shape
    place = [jax.random.randint(jax.random.fold_in(own_key, axis), (), 0, extent[axis]) for axis in range(len(extent))]
    entries = entries.at[tuple(place)].set(smallest)
    longest = extent.index(max(extent))
    place[longest] = (place[longest] + 1) % extent[longest]
    return entries.at[tuple(place)].set(largest)


def block_levels(rng, extent, shards, low, high):
    def one(position, shards_of):
        steps = jax.random.uniform(jax.random.fold_in(jax.random.fold_in(rng, 6), position), (shards_of,), jnp.float32, low / len(shards), high / len(shards))
        return jnp.repeat(jnp.exp(steps), extent[position] // shards_of).reshape((-1,) + (1,) * (len(extent) - position - 1))

    loudness = one(*shards[0])
    for cut in shards[1:]:
        loudness = loudness * one(*cut)
    return loudness


def setup_inputs(seed: int = 0, part: int = 0) -> dict:
    key_of = jax.random.split(jax.random.key(seed), 5)
    own_keys = jax.random.split(jax.random.fold_in(key_of[4], part), 5)
    phase_field = jnp.clip(jax.random.uniform(own_keys[0], (NZ, NY, NX), jnp.float32, -1.1, 1.1) * block_levels(own_keys[0], (NZ, NY, NX), ((0, 4), (1, 2), (2, 2)), -0.4, 0.0), -1.1, 1.1)
    solute_field = jnp.clip(-1.0 + 1.2 * jax.random.uniform(own_keys[1], (NZ, NY, NX), jnp.float32) ** block_levels(own_keys[1], (NZ, NY, NX), ((0, 4), (1, 2), (2, 2)), -0.2, 0.2), -1.0, 0.2)
    shift_step = jax.random.randint(own_keys[2], (1,), 0, ITERS - 1).astype(jnp.int32)
    inflow_seed = set_ends(jax.random.randint(own_keys[3], (NY, NX), 0, 1024), jax.random.fold_in(own_keys[3], 1), 0, 1023).astype(jnp.int32)
    return dict(phase_field=phase_field, solute_field=solute_field, shift_step=shift_step, inflow_seed=inflow_seed)


partition = 0.15
coupling = 2.0
diffusion = 2.0
spacing_sq = 0.64
time_step = 0.025
gradient_scale = 1.2
drift_rate = 0.01
seed_levels = 1024.0


def neighbours(side_pad, growth_pad):
    return [growth_pad[:, :-2], growth_pad[:, 2:],
            side_pad[:, :, :-2, 1:-1], side_pad[:, :, 2:, 1:-1],
            side_pad[:, :, 1:-1, :-2], side_pad[:, :, 1:-1, 2:]]


def advance(center, nearby, temper):
    phases = center[0]
    solutes = center[1]
    laplace = -6.0 * phases
    for entry in nearby:
        laplace = laplace + entry[0]
    laplace = laplace / spacing_sq
    slowing = 1.0 - (1.0 - partition) * temper
    driving = laplace + phases - phases * phases * phases - coupling * (1.0 - phases * phases) ** 2 * (solutes + temper)
    growth_rate = driving / slowing
    clipped = jnp.clip(phases, -1.0, 1.0)
    mobile = 0.5 * (1.0 - clipped)
    current = jnp.zeros_like(phases)
    for entry in nearby:
        near_mobile = 0.5 * (1.0 - jnp.clip(entry[0], -1.0, 1.0))
        current = current + 0.5 * (mobile + near_mobile) * (entry[1] - solutes)
    current = current * (diffusion / spacing_sq)
    weight = 0.5 * (1.0 + partition - (1.0 - partition) * clipped)
    solute_rate = (current + 0.5 * (1.0 + (1.0 - partition) * solutes) * growth_rate) / weight
    return jnp.stack([phases + time_step * growth_rate, solutes + time_step * solute_rate])


def reference(phase_field, solute_field, shift_step, inflow_seed):
    planes = phase_field.shape[0]
    frame_step = shift_step[0]
    inflow = inflow_seed.astype(jnp.float32) / seed_levels - 1.0
    top_pair = jnp.stack([jnp.full_like(inflow, -1.0), inflow])[:, None]
    fields = jnp.stack([phase_field, solute_field])
    heights = jnp.arange(planes).astype(jnp.float32)[:, None, None]
    for step_index in range(ITERS):
        window = jnp.pad(fields, ((0, 0), (1, 1), (0, 0), (0, 0)), mode="edge")
        side_pad = jnp.pad(fields, ((0, 0), (0, 0), (1, 1), (1, 1)), mode="wrap")
        nearby = neighbours(side_pad, window)
        shifts = (frame_step < step_index).astype(jnp.float32)
        temper = gradient_scale * ((heights + shifts + 0.5) / planes - 0.5) - drift_rate * step_index
        fields = advance(fields, nearby, temper)
        if step_index < ITERS - 1:
            shifted = jnp.concatenate([fields[:, 1:], top_pair], 1)
            fields = jnp.where(frame_step == step_index, shifted, fields)
    return fields[0], fields[1]
```

```python
import functools

import jax
import jax.numpy as jnp
from jax import lax
from jax.experimental import pallas as pl
from jax.experimental.pallas import tpu as pltpu
from jax.sharding import PartitionSpec as P

ITERS = 3
LANES = 128
SUBLANES = 8

partition = 0.15
coupling = 2.0
diffusion = 2.0
spacing_sq = 0.64
time_step = 0.025
gradient_scale = 1.2
drift_rate = 0.01
seed_levels = 1024.0

BELOW = ITERS - 1
ABOVE = ITERS + 1
RIMMED = ITERS
F32 = jnp.float32


def ring(size, by):
    return [(i, (i + by) % size) for i in range(size)]


def chain(size, by):
    return [(i, i + by) for i in range(size) if 0 <= i + by < size]


def lane_of(shape):
    return lax.broadcasted_iota(jnp.int32, shape, len(shape) - 1)


def row_of(shape):
    return lax.broadcasted_iota(jnp.int32, shape, len(shape) - 2)


def level(seed):
    return seed.astype(F32) / seed_levels - 1.0


def whole(shape):
    return pl.BlockSpec(shape, lambda _: (0,) * len(shape))


def at_block(shape, index):
    return pl.BlockSpec(shape, lambda _: index)


def cost(count):
    return pl.CostEstimate(flops=count, bytes_accessed=4 * count, transcendentals=0)


def sides_kernel(planes, phi_a, phi_b, sol_a, sol_b, seed_a, seed_b, out):
    keep = lane_of(phi_a.shape[1:]) < LANES // 2
    for k in range(planes):
        out[k] = jnp.where(keep, phi_a[k], phi_b[k])
        out[planes + k] = jnp.where(keep, sol_a[k], sol_b[k])
    out[2 * planes] = level(jnp.where(keep, seed_a[...], seed_b[...]))


def pack_sides(phi, sol, seed):
    planes, rows, cols = phi.shape
    last = cols // LANES - 1
    edge = (planes, rows, LANES)
    return pl.pallas_call(
        functools.partial(sides_kernel, planes),
        out_shape=jax.ShapeDtypeStruct((2 * planes + 1, rows, LANES), F32),
        in_specs=[
            at_block(edge, (0, 0, 0)),
            at_block(edge, (0, 0, last)),
            at_block(edge, (0, 0, 0)),
            at_block(edge, (0, 0, last)),
            at_block((rows, LANES), (0, 0)),
            at_block((rows, LANES), (0, last)),
        ],
        out_specs=whole((2 * planes + 1, rows, LANES)),
        grid=(1,),
        cost_estimate=cost((2 * planes + 1) * rows * LANES),
        name="pack_sides",
    )(phi, phi, sol, sol, seed, seed)


def rows_kernel(planes, cols, phi_a, phi_b, sol_a, sol_b, seed_a, seed_b, side_a, side_b, out):
    keep = row_of((SUBLANES, cols)) < SUBLANES // 2
    for k in range(planes):
        out[k, :, :cols] = jnp.where(keep, phi_a[k], phi_b[k])
        out[planes + k, :, :cols] = jnp.where(keep, sol_a[k], sol_b[k])
    out[2 * planes, :, :cols] = level(jnp.where(keep, seed_a[...], seed_b[...]))
    keep = row_of((SUBLANES, LANES)) < SUBLANES // 2
    for k in range(2 * planes + 1):
        out[k, :, cols:] = jnp.where(keep, side_a[k], side_b[k])


def pack_rows(phi, sol, seed, side):
    planes, rows, cols = phi.shape
    last = rows // SUBLANES - 1
    edge = (planes, SUBLANES, cols)
    count = 2 * planes + 1
    return pl.pallas_call(
        functools.partial(rows_kernel, planes, cols),
        out_shape=jax.ShapeDtypeStruct((count, SUBLANES, cols + LANES), F32),
        in_specs=[
            at_block(edge, (0, 0, 0)),
            at_block(edge, (0, last, 0)),
            at_block(edge, (0, 0, 0)),
            at_block(edge, (0, last, 0)),
            at_block((SUBLANES, cols), (0, 0)),
            at_block((SUBLANES, cols), (last, 0)),
            at_block((count, SUBLANES, LANES), (0, 0, 0)),
            at_block((count, SUBLANES, LANES), (0, last, 0)),
        ],
        out_specs=whole((count, SUBLANES, cols + LANES)),
        grid=(1,),
        cost_estimate=cost(count * SUBLANES * (cols + LANES)),
        name="pack_rows",
    )(phi, phi, sol, sol, seed, seed, side, side)


def put_row_tile(out, place, tile):
    for t in range(tile.shape[1] // LANES):
        start = (place * (tile.shape[1] // LANES) + t) * SUBLANES
        out[start : start + SUBLANES, :] = tile[:, t * LANES : (t + 1) * LANES]


def get_row_tile(ref, place, width):
    tiles = width // LANES
    return [
        ref[(place * tiles + t) * SUBLANES : (place * tiles + t + 1) * SUBLANES, :]
        for t in range(tiles)
    ]


LANE_STEP = 2 * SUBLANES


def rims_kernel(planes, cross, side, down, up):
    half = SUBLANES // 2
    rows_iota = row_of(cross.shape[1:])
    lanes_iota = lane_of(side.shape[1:])

    def rows_pair(first, second):
        mixed = pltpu.roll(cross[second], half, 0)
        inner = (rows_iota == half - 1) | (rows_iota == half)
        return jnp.where(inner, mixed, cross[first])

    def rows_two(first, second):
        mixed = pltpu.roll(cross[second], half, 0)
        inner = (rows_iota >= half - 2) & (rows_iota < half + 2)
        return jnp.where(inner, mixed, cross[first])

    def columns(entries):
        packed = side[entries[0]]
        for k, entry in enumerate(entries[1:], 1):
            moved = pltpu.roll(side[entry], k * LANE_STEP, 1)
            near = (lanes_iota >= k * LANE_STEP - half) & (lanes_iota < k * LANE_STEP + half)
            packed = jnp.where(near, moved, packed)
        return packed

    put_row_tile(down, 0, rows_pair(0, 2))
    put_row_tile(down, 1, rows_pair(planes, planes + 2))
    put_row_tile(down, 2, rows_two(1, planes + 1))
    start = down.shape[0] - side.shape[1]
    down[start:, :] = columns([0, planes, 1, planes + 1, 2, planes + 2])
    put_row_tile(up, 0, rows_pair(planes - 1, 2 * planes - 1))
    start = up.shape[0] - side.shape[1]
    up[start:, :] = columns([planes - 1, 2 * planes - 1])


def pack_rims(planes, cross, side):
    tiles = cross.shape[2] // LANES
    rows = side.shape[1]
    down = (3 * tiles * SUBLANES + rows, LANES)
    up = (tiles * SUBLANES + rows, LANES)
    return pl.pallas_call(
        functools.partial(rims_kernel, planes),
        out_shape=(jax.ShapeDtypeStruct(down, F32), jax.ShapeDtypeStruct(up, F32)),
        in_specs=[whole(cross.shape), whole(side.shape)],
        out_specs=(whole(down), whole(up)),
        grid=(1,),
        cost_estimate=cost(down[0] * LANES),
        name="pack_rims",
    )(cross, side)


def evolve_kernel(
    planes,
    grid_planes,
    shift_ref,
    where_ref,
    phi_in,
    sol_in,
    phi_up,
    sol_up,
    lows,
    side,
    cross,
    rim_down,
    rim_up,
    seed,
    phi_out,
    sol_out,
    phi_a,
    sol_a,
    mob_a,
    mix_a,
    phi_b,
    sol_b,
    mob_b,
    mix_b,
    sol_top,
    rims_d,
    rims_u,
    levels,
    sems,
):
    _, rows, cols = phi_in.shape
    wide = cols + LANES
    strips = rows // SUBLANES
    base = BELOW
    top = base + planes
    half = SUBLANES // 2
    count = top + ABOVE
    body = (pl.ds(0, rows), pl.ds(0, cols))
    edge = (pl.ds(0, rows), pl.ds(cols, LANES))
    last = (pl.ds(rows, SUBLANES), pl.ds(0, wide))
    moves = []

    def move(source, target):
        copy = pltpu.make_async_copy(source, target, sems.at[len(moves)])
        copy.start()
        moves.append(copy)

    own = pl.ds(base, planes)
    move(phi_in, phi_a.at[(own, *body)])
    move(sol_in, sol_a.at[(own, *body)])
    move(phi_up.at[pl.ds(0, ABOVE)], phi_a.at[(pl.ds(top, ABOVE), *body)])
    move(sol_up.at[pl.ds(0, ABOVE)], sol_a.at[(pl.ds(top, ABOVE), *body)])
    move(lows.at[pl.ds(0, BELOW)], phi_a.at[(pl.ds(0, BELOW), *body)])
    move(lows.at[pl.ds(BELOW, BELOW)], sol_a.at[(pl.ds(0, BELOW), *body)])
    move(side.at[pl.ds(0, planes)], phi_a.at[(own, *edge)])
    move(side.at[pl.ds(planes, planes)], sol_a.at[(own, *edge)])
    move(side.at[2 * planes], sol_top.at[edge])
    move(cross.at[pl.ds(0, planes)], phi_a.at[(own, *last)])
    move(cross.at[pl.ds(planes, planes)], sol_a.at[(own, *last)])
    move(cross.at[2 * planes], sol_top.at[last])
    move(rim_down, rims_d)
    move(rim_up, rims_u)
    move(seed, levels)
    for copy in moves:
        copy.wait()

    rowsplit = row_of((SUBLANES, LANES))

    def put_rows(ref, plane, tiles, turn):
        for t, tile in enumerate(tiles):
            lanes = slice(t * LANES, (t + 1) * LANES)
            ref[plane, rows : rows + SUBLANES, lanes] = pltpu.roll(tile, half, 0) if turn else tile

    def put_columns(ref, plane, packed, k):
        turned = pltpu.roll(packed, LANES - k * LANE_STEP, 1) if k else packed
        ref[plane, 0:rows, cols:] = turned

    first = get_row_tile(rims_d, 0, wide)
    put_rows(phi_a, top, first, False)
    put_rows(phi_a, top + 2, first, True)
    first = get_row_tile(rims_d, 1, wide)
    put_rows(sol_a, top, first, False)
    put_rows(sol_a, top + 2, first, True)
    first = get_row_tile(rims_d, 2, wide)
    put_rows(phi_a, top + 1, first, False)
    put_rows(sol_a, top + 1, first, True)
    packed = rims_d[rims_d.shape[0] - rows :, :]
    for k, (ref, plane) in enumerate(
        [(phi_a, 0), (sol_a, 0), (phi_a, 1), (sol_a, 1), (phi_a, 2), (sol_a, 2)]
    ):
        put_columns(ref, top + plane, packed, k)
    first = get_row_tile(rims_u, 0, wide)
    put_rows(phi_a, base - 1, first, False)
    put_rows(sol_a, base - 1, first, True)
    packed = rims_u[rims_u.shape[0] - rows :, :]
    put_columns(phi_a, base - 1, packed, 0)
    put_columns(sol_a, base - 1, packed, 1)

    shift = shift_ref[0]
    grow_index = where_ref[0]
    at_bottom = where_ref[1] == 1
    at_top = where_ref[2] == 1

    def derive(phi, sol):
        mobile = 1.0 - jnp.clip(phi, -1.0, 1.0)
        return mobile, mobile * sol

    @pl.loop(0, count)
    def _(e):
        for r in range(strips + 1):
            at = (e, slice(r * SUBLANES, (r + 1) * SUBLANES), slice(None))
            mob_a[at], mix_a[at] = derive(phi_a[at], sol_a[at])

    @pl.when(at_top)
    def _():
        sol_top[0:rows, 0:cols] = level(levels[...])

    def bring_top(phi, sol, mob, mix):
        for r in range(strips + 1):
            at = slice(r * SUBLANES, (r + 1) * SUBLANES)
            value = sol_top[at, :]
            phi[top, at, :] = jnp.full((SUBLANES, wide), -1.0, F32)
            sol[top, at, :] = value
            mob[top, at, :] = jnp.full((SUBLANES, wide), 2.0, F32)
            mix[top, at, :] = 2.0 * value

    def step_plane(step, source, target, e, full):
        phi, sol, mob, mix = source
        moved = shift < step
        low_end = jnp.where(moved, base + 1, base)
        high_end = jnp.where(moved, top, top - 1)
        lower = jnp.where(at_bottom & (e == low_end), e, e - 1)
        upper = jnp.where(at_top & (e == high_end), e, e + 1)
        height = (grow_index * planes + e - base).astype(F32)
        height = jnp.broadcast_to(height, (SUBLANES, LANES))
        temper = gradient_scale * ((height + 0.5) * (1.0 / grid_planes) - 0.5) - drift_rate * step
        pace = time_step / (1.0 - (1.0 - partition) * temper)
        width = wide if full else cols
        across = width // LANES
        spread = lambda v: jnp.concatenate([v] * across, axis=1)
        temper, pace = spread(temper), spread(pace)
        pull = pace * (1.0 / spacing_sq)
        drive = pace * coupling
        rest = pull * 6.0
        kappa = 0.25 * diffusion * time_step / spacing_sq
        rowid = row_of((SUBLANES, wide))
        heads = rowid == 0
        tails = rowid == SUBLANES - 1
        for r in range(strips + (1 if full else 0)):
            before = (r + strips) % (strips + 1)
            after = (r + 1) % (strips + 1)
            cut = lambda k: slice(k * SUBLANES, (k + 1) * SUBLANES)

            def around(ref):
                mid = ref[e, cut(r), :]
                prev = ref[e, cut(before), :]
                nxt = ref[e, cut(after), :]
                rowsum = pltpu.roll(jnp.where(tails, prev, mid), 1, 0)
                rowsum = rowsum + pltpu.roll(jnp.where(heads, nxt, mid), SUBLANES - 1, 0)
                colsum = pltpu.roll(mid, 1, 1) + pltpu.roll(mid, wide - 1, 1)
                total = rowsum[:, :width] + colsum[:, :width]
                total = total + ref[lower, cut(r), :width] + ref[upper, cut(r), :width]
                return mid[:, :width], total

            p, sum_p = around(phi)
            u, sum_u = around(sol)
            m, sum_m = around(mob)
            _, sum_x = around(mix)
            well = 1.0 - p * p
            gain = pull * sum_p + p * (pace * well - rest) - drive * (well * well) * (u + temper)
            new_p = p + gain
            flow = m * sum_u + sum_x - u * (6.0 * m + sum_m)
            weight = partition + 0.5 * (1.0 - partition) * m
            change = kappa * flow + (0.5 + 0.5 * (1.0 - partition) * u) * gain
            new_u = u + change / weight
            target(e, cut(r), width, new_p, new_u)

    first = (phi_a, sol_a, mob_a, mix_a)
    second = (phi_b, sol_b, mob_b, mix_b)

    def into(refs):
        def write(e, at, width, new_p, new_u):
            mobile, mixed = derive(new_p, new_u)
            for ref, value in zip(refs, (new_p, new_u, mobile, mixed)):
                ref[e, at, :width] = value

        return write

    def finish(e, at, width, new_p, new_u):
        phi_out[e - base - 1, at, :] = new_p
        sol_out[e - base - 1, at, :] = new_u

    @pl.loop(base, top + 2)
    def _(e):
        step_plane(0, first, into(second), e, True)

    step_plane(0, first, into(second), base - 1, False)
    step_plane(0, first, into(second), top + 2, False)

    @pl.when(at_top & (shift == 0))
    def _():
        bring_top(*second)

    @pl.loop(base + 1, top + 1)
    def _(e):
        step_plane(1, second, into(first), e, True)

    step_plane(1, second, into(first), base, False)
    step_plane(1, second, into(first), top + 1, False)

    @pl.when(at_top & (shift == 1))
    def _():
        bring_top(*first)

    @pl.loop(base + 1, top + 1)
    def _(e):
        step_plane(2, first, finish, e, False)


def evolve(grid_planes, shift, where, phi, sol, phi_up, sol_up, lows, side, cross, down, up, seed):
    planes, rows, cols = phi.shape
    state = (planes + BELOW + ABOVE, rows + SUBLANES, cols + LANES)
    block = jax.ShapeDtypeStruct(phi.shape, F32)
    hbm = pl.BlockSpec(memory_space=pl.ANY)
    smem = pl.BlockSpec(memory_space=pltpu.SMEM)
    return pl.pallas_call(
        functools.partial(evolve_kernel, planes, grid_planes),
        out_shape=(block, block),
        in_specs=[smem, smem] + [hbm] * 10,
        out_specs=(whole(phi.shape), whole(phi.shape)),
        scratch_shapes=[pltpu.VMEM(state, F32)] * 8
        + [
            pltpu.VMEM(state[1:], F32),
            pltpu.VMEM(down.shape, F32),
            pltpu.VMEM(up.shape, F32),
            pltpu.VMEM(seed.shape, jnp.int32),
            pltpu.SemaphoreType.DMA((15,)),
        ],
        grid=(1,),
        cost_estimate=cost(3 * 64 * phi.size),
        name="evolve",
    )(shift, where, phi, sol, phi_up, sol_up, lows, side, cross, down, up, seed)


def swap_edges(message, axis, keep):
    size = lax.axis_size(axis)
    if size <= 2:
        return lax.ppermute(message, axis, ring(size, 1))
    after = lax.ppermute(message, axis, ring(size, -1))
    before = lax.ppermute(message, axis, ring(size, 1))
    return jnp.where(keep, after, before)


def shards(phi, sol, shift_step, seed):
    planes, rows, cols = phi.shape
    size = lax.axis_size("grow")
    index = lax.axis_index("grow")
    where = jnp.stack([index, index == 0, index == size - 1]).astype(jnp.int32)
    fall = chain(size, -1)
    rise = chain(size, 1)
    phi_up = lax.ppermute(phi, "grow", fall)
    sol_up = lax.ppermute(sol, "grow", fall)
    lows = jnp.concatenate([phi[planes - BELOW :], sol[planes - BELOW :]])
    lows = lax.ppermute(lows, "grow", rise)
    side = pack_sides(phi, sol, seed)
    side = swap_edges(side, "side", lane_of(side.shape) < LANES // 2)
    cross = pack_rows(phi, sol, seed, side)
    cross = swap_edges(cross, "cross", row_of(cross.shape) < SUBLANES // 2)
    down, up = pack_rims(planes, cross, side)
    down = lax.ppermute(down, "grow", fall)
    up = lax.ppermute(up, "grow", rise)
    return evolve(
        planes * size, shift_step, where, phi, sol, phi_up, sol_up, lows, side, cross, down, up, seed
    )


def solution(mesh):
    return jax.shard_map(
        shards,
        mesh=mesh,
        in_specs=(
            P(("groups", "grow"), "cross", "side"),
            P(("groups", "grow"), "cross", "side"),
            P("groups"),
            P(("groups", "cross"), "side"),
        ),
        out_specs=(P(("groups", "grow"), "cross", "side"), P(("groups", "grow"), "cross", "side")),
        check_vma=False,
    )
```

```python
import functools

import jax
import jax.numpy as jnp
from jax import lax
from jax.experimental import pallas as pl
from jax.experimental.pallas import tpu as pltpu
from jax.sharding import PartitionSpec as P


ITERS = 3
LANES = 128
SUBLANES = 8

partition = 0.15
coupling = 2.0
diffusion = 2.0
spacing_sq = 0.64
time_step = 0.025
gradient_scale = 1.2
drift_rate = 0.01
seed_levels = 1024.0

BELOW = ITERS - 1
ABOVE = ITERS + 1
RIMMED = ITERS
F32 = jnp.float32


def ring(size, by):
    return [(i, (i + by) % size) for i in range(size)]


def chain(size, by):
    return [(i, i + by) for i in range(size) if 0 <= i + by < size]


def lane_of(shape):
    return lax.broadcasted_iota(jnp.int32, shape, len(shape) - 1)


def row_of(shape):
    return lax.broadcasted_iota(jnp.int32, shape, len(shape) - 2)


def level(seed):
    return seed.astype(F32) / seed_levels - 1.0


VMEM = pl.BlockSpec(memory_space=pltpu.VMEM)
HBM = pl.BlockSpec(memory_space=pltpu.HBM)
SMEM = pl.BlockSpec(memory_space=pltpu.SMEM)
HALF = SUBLANES // 2
LANE_STEP = 2 * SUBLANES


def cost(count):
    return pl.CostEstimate(flops=count, bytes_accessed=4 * count, transcendentals=0)


def in_hbm(x):
    return pltpu.with_memory_space_constraint(x, pltpu.HBM)


def array(*shape):
    return jax.ShapeDtypeStruct(shape, F32)


def start_all(sems, pairs):
    copies = []
    for k, (source, target) in enumerate(pairs):
        copies.append(pltpu.make_async_copy(source, target, sems.at[k]))
        copies[-1].start()
    return copies


def guest_turns(k):
    return (HALF + k, HALF - k)


def edges_kernel(planes, phi, sol, seed, side, cross, lows, cols, rows, seed_cols, seed_rows, sems):
    depth, width = phi.shape[1:]
    left, right = pl.ds(0, LANES), pl.ds(width - LANES, LANES)
    first, last = pl.ds(0, SUBLANES), pl.ds(depth - SUBLANES, SUBLANES)
    kept = pl.ds(planes - BELOW, BELOW)
    copies = start_all(
        sems,
        [
            (phi.at[:, :, left], cols.at[0]),
            (phi.at[:, :, right], cols.at[1]),
            (sol.at[:, :, left], cols.at[2]),
            (sol.at[:, :, right], cols.at[3]),
            (seed.at[:, left], seed_cols.at[0]),
            (seed.at[:, right], seed_cols.at[1]),
            (phi.at[:, first, :], rows.at[0]),
            (phi.at[:, last, :], rows.at[1]),
            (sol.at[:, first, :], rows.at[2]),
            (sol.at[:, last, :], rows.at[3]),
            (seed.at[first, :], seed_rows.at[0]),
            (seed.at[last, :], seed_rows.at[1]),
            (phi.at[kept], lows.at[pl.ds(0, BELOW)]),
            (sol.at[kept], lows.at[pl.ds(BELOW, BELOW)]),
        ],
    )
    for copy in copies[:6]:
        copy.wait()
    keep = lane_of((depth, LANES)) < LANES // 2
    for k in range(planes):
        side[k] = jnp.where(keep, cols[0, k], cols[1, k])
        side[planes + k] = jnp.where(keep, cols[2, k], cols[3, k])
    side[2 * planes] = level(jnp.where(keep, seed_cols[0], seed_cols[1]))
    for copy in copies[6:]:
        copy.wait()
    rowid = row_of((SUBLANES, width))
    keep = rowid < HALF

    def edge(field, k):
        return jnp.where(keep, rows[2 * field, k], rows[2 * field + 1, k])

    for field in range(2):
        guest = edge(field, planes - 1)
        for k in range(planes - 1):
            cross[field * (planes - 1) + k] = host(rowid, edge(field, k), guest, k)
    cross[2 * (planes - 1)] = level(jnp.where(keep, seed_rows[0], seed_rows[1]))


def host(rowid, tile, guest, k):
    low, high = guest_turns(k)
    if k >= RIMMED:
        return tile
    tile = jnp.where(rowid == HALF - 1, pltpu.roll(guest, low, 0), tile)
    return jnp.where(rowid == HALF, pltpu.roll(guest, high, 0), tile)


def hosted(rowid, tiles):
    guest = None
    for k in range(RIMMED):
        low, high = guest_turns(k)
        part = pltpu.roll(tiles[k], SUBLANES - low, 0)
        guest = part if guest is None else jnp.where(rowid == SUBLANES - 1 - k, part, guest)
        part = pltpu.roll(tiles[k], SUBLANES - high, 0)
        guest = jnp.where(rowid == k, part, guest)
    return guest


def pack_edges(phi, sol, seed):
    planes, rows, cols = phi.shape
    return pl.pallas_call(
        functools.partial(edges_kernel, planes),
        out_shape=(
            array(2 * planes + 1, rows, LANES),
            array(2 * planes - 1, SUBLANES, cols),
            array(2 * BELOW, rows, cols),
        ),
        in_specs=[HBM, HBM, HBM],
        out_specs=(VMEM, VMEM, VMEM),
        scratch_shapes=[
            pltpu.VMEM((4, planes, rows, LANES), F32),
            pltpu.VMEM((4, planes, SUBLANES, cols), F32),
            pltpu.VMEM((2, rows, LANES), jnp.int32),
            pltpu.VMEM((2, SUBLANES, cols), jnp.int32),
            pltpu.SemaphoreType.DMA((14,)),
        ],
        cost_estimate=cost(phi.size),
        compiler_params=pltpu.CompilerParams(vmem_limit_bytes=4 << 20),
        name="pack_edges",
    )(*(in_hbm(x) for x in (phi, sol, seed)))


def rows_kernel(planes, main, side, out):
    width = main.shape[2]
    out[:, :, :width] = main[...]
    rowid = row_of((SUBLANES, LANES))
    keep = rowid < HALF
    depth = side.shape[1]

    def edge(entry):
        return jnp.where(keep, side[entry, :SUBLANES], side[entry, depth - SUBLANES :])

    for field in range(2):
        guest = edge((field + 1) * planes - 1)
        for k in range(planes - 1):
            tile = host(rowid, edge(field * planes + k), guest, k)
            out[field * (planes - 1) + k, :, width:] = tile
    out[2 * (planes - 1), :, width:] = edge(2 * planes)


def pack_rows(planes, main, side):
    count, _, cols = main.shape
    return pl.pallas_call(
        functools.partial(rows_kernel, planes),
        out_shape=array(count, SUBLANES, cols + LANES),
        in_specs=[VMEM, VMEM],
        out_specs=VMEM,
        cost_estimate=cost(main.size),
        compiler_params=pltpu.CompilerParams(vmem_limit_bytes=2 << 20),
        name="pack_rows",
    )(main, side)


def put_row_tile(out, place, tile):
    tiles = tile.shape[1] // LANES
    for t in range(tiles):
        start = (place * tiles + t) * SUBLANES
        out[start : start + SUBLANES, :] = tile[:, t * LANES : (t + 1) * LANES]


def get_row_tile(ref, place, tiles):
    return [
        ref[(place * tiles + t) * SUBLANES : (place * tiles + t + 1) * SUBLANES, :]
        for t in range(tiles)
    ]


def rims_kernel(planes, cross, side, down, up):
    other = planes - 1
    rowid = row_of(cross.shape[1:])
    lanes = lane_of(side.shape[1:])
    inner = (rowid == HALF - 1) | (rowid == HALF)
    middle = (rowid >= HALF - 2) & (rowid < HALF + 2)
    turn = lambda tile: pltpu.roll(tile, HALF, 0)

    def columns(entries):
        packed = side[entries[0]]
        for k, entry in enumerate(entries[1:], 1):
            moved = pltpu.roll(side[entry], k * LANE_STEP, 1)
            near = (lanes >= k * LANE_STEP - HALF) & (lanes < k * LANE_STEP + HALF)
            packed = jnp.where(near, moved, packed)
        return packed

    put_row_tile(down, 0, jnp.where(inner, turn(cross[2]), cross[0]))
    put_row_tile(down, 1, jnp.where(inner, turn(cross[other + 2]), cross[other]))
    put_row_tile(down, 2, jnp.where(middle, turn(cross[other + 1]), cross[1]))
    start = down.shape[0] - side.shape[1]
    down[start:, :] = columns([0, planes, 1, planes + 1, 2, planes + 2])
    put_row_tile(up, 0, jnp.where(inner, cross[other], turn(cross[0])))
    start = up.shape[0] - side.shape[1]
    up[start:, :] = columns([planes - 1, 2 * planes - 1])


def pack_rims(planes, cross, side):
    tiles = cross.shape[2] // LANES
    rows = side.shape[1]
    down = array(3 * tiles * SUBLANES + rows, LANES)
    up = array(tiles * SUBLANES + rows, LANES)
    return pl.pallas_call(
        functools.partial(rims_kernel, planes),
        out_shape=(down, up),
        in_specs=[VMEM, VMEM],
        out_specs=(VMEM, VMEM),
        cost_estimate=cost(down.size),
        compiler_params=pltpu.CompilerParams(vmem_limit_bytes=2 << 20),
        name="pack_rims",
    )(cross, side)


def mobility(phi):
    return 1.0 - jnp.clip(phi, -1.0, 1.0)


class Field:
    def __init__(self, phi, sol, mob, planes):
        self.phi, self.sol, self.mob = phi, sol, mob
        self.planes = planes
        self.tiles = phi.shape[1]
        self.rows = phi.shape[2] - 2 * SUBLANES
        self.base = BELOW
        self.top = BELOW + planes

    def put(self, e, t, at, p, u):
        self.phi[e, t, at, :] = p
        self.sol[e, t, at, :] = u
        self.mob[e, t, at, :] = mobility(p)

    def put_block(self, e, phi, sol, k, j):
        for t in range(self.tiles - 1):
            lanes = slice(t * LANES, (t + 1) * LANES)
            at = slice(SUBLANES, SUBLANES + self.rows)
            self.put(e, t, at, phi[k, :, lanes], sol[j, :, lanes])

    def put_columns(self, e, p, u):
        self.put(e, self.tiles - 1, slice(SUBLANES, SUBLANES + self.rows), p, u)

    def put_rows(self, e, p, u):
        for t in range(self.tiles):
            for start in (0, SUBLANES + self.rows):
                self.put(e, t, slice(start, start + SUBLANES), p[t], u[t])


def ends(step, shift, field, e):
    grow_index = lax.axis_index("grow")
    at_bottom = grow_index == 0
    at_top = grow_index == lax.axis_size("grow") - 1
    moved = shift < step
    low_end = jnp.where(moved, field.base + 1, field.base)
    high_end = jnp.where(moved, field.top, field.top - 1)
    lower = jnp.where(at_bottom & (e == low_end), e, e - 1)
    upper = jnp.where(at_top & (e == high_end), e, e + 1)
    return lower, upper


def step_plane(step, shift, source, e, halo, write):
    lower, upper = ends(step, shift, source, e)
    planes = source.planes
    grid_planes = planes * lax.axis_size("grow")
    height = (lax.axis_index("grow") * planes + e - source.base).astype(F32)
    height = jnp.broadcast_to(height, (SUBLANES, LANES))
    temper = gradient_scale * ((height + 0.5) * (1.0 / grid_planes) - 0.5) - drift_rate * step
    pace = time_step / (1.0 - (1.0 - partition) * temper)
    kappa = 0.25 * diffusion * time_step / spacing_sq
    pull = pace * (1.0 / spacing_sq)
    drive = pace * coupling
    rest = pull * 6.0
    tiles = source.tiles
    lanes = lane_of((SUBLANES, LANES))
    heads = lanes == 0
    tails = lanes == LANES - 1
    rows = source.rows + 2 * halo
    outputs = tiles if halo else tiles - 1
    for r in range(-(-rows // SUBLANES)):
        start = SUBLANES - halo + r * SUBLANES

        def load(ref, t, plane=e, by=0):
            return ref[plane, t, start + by : start + by + SUBLANES, :]

        def after(values, t):
            return pltpu.roll(jnp.where(heads, values[(t + 1) % tiles], values[t]), LANES - 1, 1)

        def before(values, t):
            return pltpu.roll(jnp.where(tails, values[t - 1], values[t]), 1, 1)

        p_all = [load(source.phi, t) for t in range(tiles)]
        u_all = [load(source.sol, t) for t in range(tiles)]
        m_all = [load(source.mob, t) for t in range(tiles)]
        flux = [
            (m_all[t] + after(m_all, t)) * (after(u_all, t) - u_all[t]) for t in range(tiles)
        ]
        for t in range(outputs):
            p, u, m = p_all[t], u_all[t], m_all[t]
            total = after(p_all, t) + before(p_all, t)
            flow = flux[t] - before(flux, t)
            for where in (dict(by=-1), dict(by=1), dict(plane=lower), dict(plane=upper)):
                total = total + load(source.phi, t, **where)
                other = load(source.sol, t, **where)
                flow = flow + (m + load(source.mob, t, **where)) * (other - u)
            well = 1.0 - p * p
            gain = pull * total + p * (pace * well - rest) - drive * (well * well) * (u + temper)
            weight = partition / kappa + (0.5 * (1.0 - partition) / kappa) * m
            change = flow + (0.5 / kappa + (0.5 * (1.0 - partition) / kappa) * u) * gain
            write(e, t, slice(start, start + SUBLANES), p + gain, u + change / weight)


def early_kernel(planes, shift_ref, phi, sol, phi_up, sol_up, side, cross, *rest):
    first = Field(*rest[:3], planes)
    second = Field(*rest[3:6], planes)
    own_phi, own_sol, sems = rest[6:]
    base, top, tiles = first.base, first.top, first.tiles
    copies = start_all(sems, [(phi, own_phi), (sol, own_sol)])
    rowid = row_of((SUBLANES, LANES))
    cut = lambda t: slice(t * LANES, (t + 1) * LANES)
    other = planes - 1
    for k in range(planes):
        first.put_columns(base + k, side[k], side[planes + k])
        if k < other:
            p = [cross[k, :, cut(t)] for t in range(tiles)]
            u = [cross[other + k, :, cut(t)] for t in range(tiles)]
        else:
            p, u = [
                [
                    hosted(rowid, [cross[f * other + j, :, cut(t)] for j in range(RIMMED)])
                    for t in range(tiles)
                ]
                for f in range(2)
            ]
        first.put_rows(base + k, p, u)
    for k in range(ABOVE):
        first.put_block(top + k, phi_up, sol_up, k, k)
    for copy in copies:
        copy.wait()
    for k in range(planes):
        first.put_block(base + k, own_phi, own_sol, k, k)

    @pl.loop(base + 1, top - 1)
    def _(e):
        step_plane(0, shift_ref[0], first, e, 2, second.put)


def late_kernel(planes, shift_ref, lows, side, cross, rim_down, rim_up, seed, *rest):
    phi_out, sol_out = rest[6:8]
    first = Field(*rest[8:11], planes)
    second = Field(*rest[11:14], planes)
    levels, phi_buf, sol_buf, sems = rest[14:]
    base, top, tiles, rows = first.base, first.top, first.tiles, first.rows
    shift = shift_ref[0]
    at_top = lax.axis_index("grow") == lax.axis_size("grow") - 1
    fetch = pltpu.make_async_copy(seed, levels, sems.at[0])
    fetch.start()
    turn = lambda group: [pltpu.roll(tile, HALF, 0) for tile in group]
    for k in range(BELOW):
        first.put_block(k, lows, lows, k, BELOW + k)
    p = get_row_tile(rim_down, 0, tiles)
    u = get_row_tile(rim_down, 1, tiles)
    first.put_rows(top, p, u)
    first.put_rows(top + 2, turn(p), turn(u))
    p = get_row_tile(rim_down, 2, tiles)
    first.put_rows(top + 1, p, turn(p))
    p = get_row_tile(rim_up, 0, tiles)
    first.put_rows(base - 1, p, turn(p))

    def spread(packed, k):
        return pltpu.roll(packed, LANES - k * LANE_STEP, 1) if k else packed

    packed = rim_down[rim_down.shape[0] - rows :, :]
    for k in range(RIMMED):
        first.put_columns(top + k, spread(packed, 2 * k), spread(packed, 2 * k + 1))
    packed = rim_up[rim_up.shape[0] - rows :, :]
    first.put_columns(base - 1, packed, spread(packed, 1))
    fetch.wait()

    def bring_top(field):
        def fill(t, at, value):
            field.put(top, t, at, jnp.full(value.shape, -1.0, F32), value)

        body = slice(SUBLANES, SUBLANES + rows)
        for t in range(tiles - 1):
            fill(t, body, level(levels[:, t * LANES : (t + 1) * LANES]))
        fill(tiles - 1, body, side[2 * planes])
        for t in range(tiles):
            value = cross[2 * (planes - 1), :, t * LANES : (t + 1) * LANES]
            fill(t, slice(0, SUBLANES), value)
            fill(t, slice(SUBLANES + rows, 2 * SUBLANES + rows), value)

    @pl.loop(0, 4)
    def _(k):
        e = jnp.where(k == 0, base, top - 2 + k)
        step_plane(0, shift, first, e, 2, second.put)

    @pl.loop(0, 2)
    def _(k):
        step_plane(0, shift, first, jnp.where(k == 0, base - 1, top + 2), 0, second.put)

    @pl.when(at_top & (shift == 0))
    def _():
        bring_top(second)

    @pl.loop(base + 1, top + 1)
    def _(e):
        step_plane(1, shift, second, e, 1, first.put)

    @pl.loop(0, 2)
    def _(k):
        step_plane(1, shift, second, jnp.where(k == 0, base, top + 1), 0, first.put)

    @pl.when(at_top & (shift == 1))
    def _():
        bring_top(first)

    def out_copy(which, j):
        buf, out = ((phi_buf, phi_out), (sol_buf, sol_out))[which]
        return pltpu.make_async_copy(buf.at[j], out.at[j], sems.at[1 + which * planes + j])

    @pl.loop(0, planes)
    def _(j):
        def finish(e, t, at, p, u):
            place = (j, slice(at.start - SUBLANES, at.stop - SUBLANES), slice(t * LANES, (t + 1) * LANES))
            phi_buf[place] = p
            sol_buf[place] = u

        step_plane(2, shift, first, j + base + 1, 0, finish)
        out_copy(0, j).start()
        out_copy(1, j).start()

    for j in range(planes):
        out_copy(0, j).wait()
        out_copy(1, j).wait()


def early(shift, phi, sol, phi_up, sol_up, side, cross):
    planes, rows, cols = phi.shape
    state = array(planes + BELOW + ABOVE, cols // LANES + 1, rows + 2 * SUBLANES, LANES)
    return pl.pallas_call(
        functools.partial(early_kernel, planes),
        out_shape=(state,) * 6,
        in_specs=[SMEM, HBM, HBM] + [VMEM] * 4,
        out_specs=(VMEM,) * 6,
        scratch_shapes=[
            pltpu.VMEM(phi.shape, F32),
            pltpu.VMEM(phi.shape, F32),
            pltpu.SemaphoreType.DMA((2,)),
        ],
        cost_estimate=cost(64 * phi.size),
        compiler_params=pltpu.CompilerParams(vmem_limit_bytes=12 << 20),
        name="early",
    )(shift, phi, sol, phi_up, sol_up, side, cross)


def late(shift, lows, side, cross, down, up, seed, state, shape):
    planes = shape[0]
    kept = tuple(jax.ShapeDtypeStruct(s.shape, s.dtype) for s in state)
    out = pl.pallas_call(
        functools.partial(late_kernel, planes),
        out_shape=(array(*shape), array(*shape)) + kept,
        in_specs=[SMEM] + [VMEM] * 5 + [HBM] + [VMEM] * 6,
        out_specs=(HBM, HBM) + (VMEM,) * 6,
        input_output_aliases={7 + k: 2 + k for k in range(6)},
        scratch_shapes=[
            pltpu.VMEM(seed.shape, jnp.int32),
            pltpu.VMEM(shape, F32),
            pltpu.VMEM(shape, F32),
            pltpu.SemaphoreType.DMA((1 + 2 * planes,)),
        ],
        cost_estimate=cost(3 * 64 * state[0].size),
        compiler_params=pltpu.CompilerParams(vmem_limit_bytes=12 << 20),
        name="late",
    )(shift, lows, side, cross, down, up, seed, *state)
    return out[0], out[1]


def swap_edges(message, axis, keep):
    size = lax.axis_size(axis)
    if size <= 2:
        return lax.ppermute(message, axis, ring(size, 1))
    after = lax.ppermute(message, axis, ring(size, -1))
    before = lax.ppermute(message, axis, ring(size, 1))
    return jnp.where(keep, after, before)


def steps(phi, sol, shift_step, seed):
    planes = phi.shape[0]
    size = lax.axis_size("grow")
    fall = chain(size, -1)
    rise = chain(size, 1)
    phi_up = lax.ppermute(phi, "grow", fall)
    sol_up = lax.ppermute(sol, "grow", fall)
    side, cross, lows = pack_edges(phi, sol, seed)
    lows = lax.ppermute(lows, "grow", rise)
    side = swap_edges(side, "side", lane_of(side.shape) < LANES // 2)
    cross = pack_rows(planes, cross, side)
    rowid = row_of(cross.shape)
    cross = swap_edges(cross, "cross", (rowid < HALF - 1) | (rowid == HALF))
    down, up = pack_rims(planes, cross, side)
    down = lax.ppermute(down, "grow", fall)
    up = lax.ppermute(up, "grow", rise)
    state = early(shift_step, phi, sol, phi_up, sol_up, side, cross)
    return late(shift_step, lows, side, cross, down, up, seed, state, phi.shape)


def solution(mesh):
    return jax.shard_map(
        steps,
        mesh=mesh,
        in_specs=(
            P(("groups", "grow"), "cross", "side"),
            P(("groups", "grow"), "cross", "side"),
            P("groups"),
            P(("groups", "cross"), "side"),
        ),
        out_specs=(P(("groups", "grow"), "cross", "side"), P(("groups", "grow"), "cross", "side")),
        check_vma=False,
    )
```

```python
import functools

import jax
import jax.numpy as jnp
from jax import lax
from jax.experimental import pallas as pl
from jax.experimental.pallas import tpu as pltpu
from jax.sharding import PartitionSpec as P


ITERS = 3
LANES = 128
SUBLANES = 8

partition = 0.15
coupling = 2.0
diffusion = 2.0
spacing_sq = 0.64
time_step = 0.025
gradient_scale = 1.2
drift_rate = 0.01
seed_levels = 1024.0

BELOW = ITERS - 1
ABOVE = ITERS + 1
RIMMED = ITERS
F32 = jnp.float32


def ring(size, by):
    return [(i, (i + by) % size) for i in range(size)]


def chain(size, by):
    return [(i, i + by) for i in range(size) if 0 <= i + by < size]


def two_way(size, lanes, even_by):
    pairs = []
    for g in range(size):
        for c in range(lanes):
            target = g + (even_by if c % 2 == 0 else -even_by)
            inside = 0 <= target < size
            pairs.append((g * lanes + c, target * lanes + c if inside else g * lanes + (c ^ 1)))
    return pairs


def lane_of(shape):
    return lax.broadcasted_iota(jnp.int32, shape, len(shape) - 1)


def row_of(shape):
    return lax.broadcasted_iota(jnp.int32, shape, len(shape) - 2)


def level(seed):
    return seed.astype(F32) / seed_levels - 1.0


VMEM = pl.BlockSpec(memory_space=pltpu.VMEM)
HBM = pl.BlockSpec(memory_space=pltpu.HBM)
SMEM = pl.BlockSpec(memory_space=pltpu.SMEM)
HALF = SUBLANES // 2
LANE_STEP = 2 * SUBLANES


def cost(count):
    return pl.CostEstimate(flops=count, bytes_accessed=4 * count, transcendentals=0)


def in_hbm(x):
    return pltpu.with_memory_space_constraint(x, pltpu.HBM)


def array(*shape):
    return jax.ShapeDtypeStruct(shape, F32)


def start_all(sems, pairs):
    copies = []
    for k, (source, target) in enumerate(pairs):
        copies.append(pltpu.make_async_copy(source, target, sems.at[k]))
        copies[-1].start()
    return copies


def guest_turns(k):
    return (HALF + k, HALF - k)


def odd_core():
    return lax.axis_index("side") % 2 == 1


def edges_kernel(planes, phi, sol, seed, side, cross, bulk_a, bulk_b, cols, rows, seed_cols, seed_rows, sems):
    depth, width = phi.shape[1:]
    left, right = pl.ds(0, LANES), pl.ds(width - LANES, LANES)
    first, last = pl.ds(0, SUBLANES), pl.ds(depth - SUBLANES, SUBLANES)
    every = slice(None)
    kept = pl.ds(planes - BELOW, BELOW)
    copies = start_all(
        sems,
        [
            (phi.at[:, :, left], cols.at[0]),
            (phi.at[:, :, right], cols.at[1]),
            (sol.at[:, :, left], cols.at[2]),
            (sol.at[:, :, right], cols.at[3]),
            (seed.at[:, left], seed_cols.at[0]),
            (seed.at[:, right], seed_cols.at[1]),
            (phi.at[:, first, :], rows.at[0]),
            (phi.at[:, last, :], rows.at[1]),
            (sol.at[:, first, :], rows.at[2]),
            (sol.at[:, last, :], rows.at[3]),
            (seed.at[first, :], seed_rows.at[0]),
            (seed.at[last, :], seed_rows.at[1]),
        ],
    )

    def fill(fall, rise):
        low, high = pl.ds(0, BELOW), pl.ds(BELOW, BELOW)
        start_all(sems.at[pl.ds(12, 3)], [(phi, fall), (phi.at[kept], rise.at[low]), (sol.at[kept], rise.at[high])])

    @pl.when(jnp.logical_not(odd_core()))
    def _():
        fill(bulk_a, bulk_b)

    @pl.when(odd_core())
    def _():
        fill(bulk_b, bulk_a)

    for copy in copies[:6]:
        copy.wait()
    keep = lane_of((depth, LANES)) < LANES // 2
    for k in range(planes):
        side[k] = jnp.where(keep, cols[0, k], cols[1, k])
        side[planes + k] = jnp.where(keep, cols[2, k], cols[3, k])
    side[2 * planes] = level(jnp.where(keep, seed_cols[0], seed_cols[1]))
    for copy in copies[6:]:
        copy.wait()
    rowid = row_of((SUBLANES, width))
    keep = rowid < HALF

    def edge(field, k):
        return jnp.where(keep, rows[2 * field, k], rows[2 * field + 1, k])

    for field in range(2):
        guest = edge(field, planes - 1)
        for k in range(planes - 1):
            cross[field * (planes - 1) + k] = host(rowid, edge(field, k), guest, k)
    cross[2 * (planes - 1)] = level(jnp.where(keep, seed_rows[0], seed_rows[1]))
    pltpu.make_async_copy(phi, bulk_a, sems.at[12]).wait()
    for k in range(2):
        part = bulk_b.at[pl.ds(k * BELOW, BELOW)]
        pltpu.make_async_copy(phi.at[kept], part, sems.at[13 + k]).wait()


def host(rowid, tile, guest, k):
    low, high = guest_turns(k)
    if k >= RIMMED:
        return tile
    tile = jnp.where(rowid == HALF - 1, pltpu.roll(guest, low, 0), tile)
    return jnp.where(rowid == HALF, pltpu.roll(guest, high, 0), tile)


def hosted(rowid, tiles):
    guest = None
    for k in range(RIMMED):
        low, high = guest_turns(k)
        part = pltpu.roll(tiles[k], SUBLANES - low, 0)
        guest = part if guest is None else jnp.where(rowid == SUBLANES - 1 - k, part, guest)
        part = pltpu.roll(tiles[k], SUBLANES - high, 0)
        guest = jnp.where(rowid == k, part, guest)
    return guest


def pack_edges(phi, sol, seed):
    planes, rows, cols = phi.shape
    return pl.pallas_call(
        functools.partial(edges_kernel, planes),
        out_shape=(
            array(2 * planes + 1, rows, LANES),
            array(2 * planes - 1, SUBLANES, cols),
            array(*phi.shape),
            array(*phi.shape),
        ),
        in_specs=[HBM, HBM, HBM],
        out_specs=(VMEM,) * 4,
        scratch_shapes=[
            pltpu.VMEM((4, planes, rows, LANES), F32),
            pltpu.VMEM((4, planes, SUBLANES, cols), F32),
            pltpu.VMEM((2, rows, LANES), jnp.int32),
            pltpu.VMEM((2, SUBLANES, cols), jnp.int32),
            pltpu.SemaphoreType.DMA((15,)),
        ],
        cost_estimate=cost(phi.size),
        compiler_params=pltpu.CompilerParams(vmem_limit_bytes=4 << 20),
        name="pack_edges",
    )(*(in_hbm(x) for x in (phi, sol, seed)))


def rows_kernel(planes, main, side, out):
    width = main.shape[2]
    out[:, :, :width] = main[...]
    rowid = row_of((SUBLANES, LANES))
    keep = rowid < HALF
    depth = side.shape[1]

    def edge(entry):
        return jnp.where(keep, side[entry, :SUBLANES], side[entry, depth - SUBLANES :])

    for field in range(2):
        guest = edge((field + 1) * planes - 1)
        for k in range(planes - 1):
            tile = host(rowid, edge(field * planes + k), guest, k)
            out[field * (planes - 1) + k, :, width:] = tile
    out[2 * (planes - 1), :, width:] = edge(2 * planes)


def pack_rows(planes, main, side):
    count, _, cols = main.shape
    return pl.pallas_call(
        functools.partial(rows_kernel, planes),
        out_shape=array(count, SUBLANES, cols + LANES),
        in_specs=[VMEM, VMEM],
        out_specs=VMEM,
        cost_estimate=cost(main.size),
        compiler_params=pltpu.CompilerParams(vmem_limit_bytes=2 << 20),
        name="pack_rows",
    )(main, side)


def put_row_tile(out, place, tile):
    tiles = tile.shape[1] // LANES
    for t in range(tiles):
        start = (place * tiles + t) * SUBLANES
        out[start : start + SUBLANES, :] = tile[:, t * LANES : (t + 1) * LANES]


def get_row_tile(ref, place, tiles):
    return [
        ref[(place * tiles + t) * SUBLANES : (place * tiles + t + 1) * SUBLANES, :]
        for t in range(tiles)
    ]


def rims_kernel(planes, cross, side, rim_a, rim_b):
    other = planes - 1
    rowid = row_of(cross.shape[1:])
    lanes = lane_of(side.shape[1:])
    inner = (rowid == HALF - 1) | (rowid == HALF)
    middle = (rowid >= HALF - 2) & (rowid < HALF + 2)
    turn = lambda tile: pltpu.roll(tile, HALF, 0)
    depth = side.shape[1]

    def columns(entries):
        packed = side[entries[0]]
        for k, entry in enumerate(entries[1:], 1):
            moved = pltpu.roll(side[entry], k * LANE_STEP, 1)
            near = (lanes >= k * LANE_STEP - HALF) & (lanes < k * LANE_STEP + HALF)
            packed = jnp.where(near, moved, packed)
        return packed

    def fill(down, up):
        put_row_tile(down, 0, jnp.where(inner, turn(cross[2]), cross[0]))
        put_row_tile(down, 1, jnp.where(inner, turn(cross[other + 2]), cross[other]))
        put_row_tile(down, 2, jnp.where(middle, turn(cross[other + 1]), cross[1]))
        down[down.shape[0] - depth :, :] = columns([0, planes, 1, planes + 1, 2, planes + 2])
        put_row_tile(up, 0, jnp.where(inner, cross[other], turn(cross[0])))
        up[up.shape[0] - depth :, :] = columns([planes - 1, 2 * planes - 1])

    @pl.when(jnp.logical_not(odd_core()))
    def _():
        fill(rim_a, rim_b)

    @pl.when(odd_core())
    def _():
        fill(rim_b, rim_a)


def pack_rims(planes, cross, side):
    rim = array(3 * cross.shape[2] // LANES * SUBLANES + side.shape[1], LANES)
    return pl.pallas_call(
        functools.partial(rims_kernel, planes),
        out_shape=(rim, rim),
        in_specs=[VMEM, VMEM],
        out_specs=(VMEM, VMEM),
        cost_estimate=cost(rim.size),
        compiler_params=pltpu.CompilerParams(vmem_limit_bytes=2 << 20),
        name="pack_rims",
    )(cross, side)


class Either:
    def __init__(self, even, odd):
        self.even, self.odd, self.shape = even, odd, even.shape

    def __getitem__(self, at):
        return jnp.where(odd_core(), self.odd[at], self.even[at])


def mobility(phi):
    return 1.0 - jnp.clip(phi, -1.0, 1.0)


class Field:
    def __init__(self, phi, sol, mob, planes):
        self.phi, self.sol, self.mob = phi, sol, mob
        self.planes = planes
        self.tiles = phi.shape[1]
        self.rows = phi.shape[2] - 2 * SUBLANES
        self.base = BELOW
        self.top = BELOW + planes

    def put(self, e, t, at, p, u):
        self.phi[e, t, at, :] = p
        self.sol[e, t, at, :] = u
        self.mob[e, t, at, :] = mobility(p)

    def put_block(self, e, phi, sol, k, j):
        for t in range(self.tiles - 1):
            lanes = slice(t * LANES, (t + 1) * LANES)
            at = slice(SUBLANES, SUBLANES + self.rows)
            self.put(e, t, at, phi[k, :, lanes], sol[j, :, lanes])

    def put_columns(self, e, p, u):
        self.put(e, self.tiles - 1, slice(SUBLANES, SUBLANES + self.rows), p, u)

    def put_rows(self, e, p, u):
        for t in range(self.tiles):
            for start in (0, SUBLANES + self.rows):
                self.put(e, t, slice(start, start + SUBLANES), p[t], u[t])


def ends(step, shift, field, e):
    grow_index = lax.axis_index("grow")
    at_bottom = grow_index == 0
    at_top = grow_index == lax.axis_size("grow") - 1
    moved = shift < step
    low_end = jnp.where(moved, field.base + 1, field.base)
    high_end = jnp.where(moved, field.top, field.top - 1)
    lower = jnp.where(at_bottom & (e == low_end), e, e - 1)
    upper = jnp.where(at_top & (e == high_end), e, e + 1)
    return lower, upper


def step_plane(step, shift, source, e, halo, write):
    lower, upper = ends(step, shift, source, e)
    planes = source.planes
    grid_planes = planes * lax.axis_size("grow")
    height = (lax.axis_index("grow") * planes + e - source.base).astype(F32)
    height = jnp.broadcast_to(height, (SUBLANES, LANES))
    temper = gradient_scale * ((height + 0.5) * (1.0 / grid_planes) - 0.5) - drift_rate * step
    pace = time_step / (1.0 - (1.0 - partition) * temper)
    kappa = 0.25 * diffusion * time_step / spacing_sq
    pull = pace * (1.0 / spacing_sq)
    drive = pace * coupling
    rest = pull * 6.0
    tiles = source.tiles
    lanes = lane_of((SUBLANES, LANES))
    heads = lanes == 0
    tails = lanes == LANES - 1
    rows = source.rows + 2 * halo
    outputs = tiles if halo else tiles - 1
    for r in range(-(-rows // SUBLANES)):
        start = SUBLANES - halo + r * SUBLANES

        def load(ref, t, plane=e, by=0):
            return ref[plane, t, start + by : start + by + SUBLANES, :]

        def after(values, t):
            return pltpu.roll(jnp.where(heads, values[(t + 1) % tiles], values[t]), LANES - 1, 1)

        def before(values, t):
            return pltpu.roll(jnp.where(tails, values[t - 1], values[t]), 1, 1)

        p_all = [load(source.phi, t) for t in range(tiles)]
        u_all = [load(source.sol, t) for t in range(tiles)]
        m_all = [load(source.mob, t) for t in range(tiles)]
        flux = [
            (m_all[t] + after(m_all, t)) * (after(u_all, t) - u_all[t]) for t in range(tiles)
        ]
        for t in range(outputs):
            p, u, m = p_all[t], u_all[t], m_all[t]
            total = after(p_all, t) + before(p_all, t)
            flow = flux[t] - before(flux, t)
            for where in (dict(by=-1), dict(by=1), dict(plane=lower), dict(plane=upper)):
                total = total + load(source.phi, t, **where)
                other = load(source.sol, t, **where)
                flow = flow + (m + load(source.mob, t, **where)) * (other - u)
            well = 1.0 - p * p
            gain = pull * total + p * (pace * well - rest) - drive * (well * well) * (u + temper)
            weight = partition / kappa + (0.5 * (1.0 - partition) / kappa) * m
            change = flow + (0.5 / kappa + (0.5 * (1.0 - partition) / kappa) * u) * gain
            write(e, t, slice(start, start + SUBLANES), p + gain, u + change / weight)


def early_kernel(planes, shift_ref, phi, sol, bulk_a, bulk_b, sol_up, side, cross, *rest):
    first = Field(*rest[:3], planes)
    second = Field(*rest[3:6], planes)
    own_phi, own_sol, sems = rest[6:]
    base, top, tiles = first.base, first.top, first.tiles
    copies = start_all(sems, [(phi, own_phi), (sol, own_sol)])
    rowid = row_of((SUBLANES, LANES))
    cut = lambda t: slice(t * LANES, (t + 1) * LANES)
    other = planes - 1
    for k in range(planes):
        first.put_columns(base + k, side[k], side[planes + k])
        if k < other:
            p = [cross[k, :, cut(t)] for t in range(tiles)]
            u = [cross[other + k, :, cut(t)] for t in range(tiles)]
        else:
            p, u = [
                [
                    hosted(rowid, [cross[f * other + j, :, cut(t)] for j in range(RIMMED)])
                    for t in range(tiles)
                ]
                for f in range(2)
            ]
        first.put_rows(base + k, p, u)
    phi_up, lows = Either(bulk_a, bulk_b), Either(bulk_b, bulk_a)
    for k in range(ABOVE):
        first.put_block(top + k, phi_up, sol_up, k, k)
    for k in range(BELOW):
        first.put_block(k, lows, lows, k, BELOW + k)
    for copy in copies:
        copy.wait()
    for k in range(planes):
        first.put_block(base + k, own_phi, own_sol, k, k)

    @pl.loop(base + 1, top - 1)
    def _(e):
        step_plane(0, shift_ref[0], first, e, 2, second.put)


def late_kernel(planes, shift_ref, side, cross, rim_a, rim_b, seed, *rest):
    phi_out, sol_out = rest[6:8]
    first = Field(*rest[8:11], planes)
    second = Field(*rest[11:14], planes)
    levels, phi_buf, sol_buf, sems = rest[14:]
    base, top, tiles, rows = first.base, first.top, first.tiles, first.rows
    shift = shift_ref[0]
    at_top = lax.axis_index("grow") == lax.axis_size("grow") - 1
    fetch = pltpu.make_async_copy(seed, levels, sems.at[0])
    fetch.start()
    turn = lambda group: [pltpu.roll(tile, HALF, 0) for tile in group]
    rim_down, rim_up = Either(rim_a, rim_b), Either(rim_b, rim_a)
    p = get_row_tile(rim_down, 0, tiles)
    u = get_row_tile(rim_down, 1, tiles)
    first.put_rows(top, p, u)
    first.put_rows(top + 2, turn(p), turn(u))
    p = get_row_tile(rim_down, 2, tiles)
    first.put_rows(top + 1, p, turn(p))
    p = get_row_tile(rim_up, 0, tiles)
    first.put_rows(base - 1, p, turn(p))

    def spread(packed, k):
        return pltpu.roll(packed, LANES - k * LANE_STEP, 1) if k else packed

    packed = rim_down[rim_down.shape[0] - rows :, :]
    for k in range(RIMMED):
        first.put_columns(top + k, spread(packed, 2 * k), spread(packed, 2 * k + 1))
    packed = rim_up[rim_up.shape[0] - rows :, :]
    first.put_columns(base - 1, packed, spread(packed, 1))
    fetch.wait()

    def bring_top(field):
        def fill(t, at, value):
            field.put(top, t, at, jnp.full(value.shape, -1.0, F32), value)

        body = slice(SUBLANES, SUBLANES + rows)
        for t in range(tiles - 1):
            fill(t, body, level(levels[:, t * LANES : (t + 1) * LANES]))
        fill(tiles - 1, body, side[2 * planes])
        for t in range(tiles):
            value = cross[2 * (planes - 1), :, t * LANES : (t + 1) * LANES]
            fill(t, slice(0, SUBLANES), value)
            fill(t, slice(SUBLANES + rows, 2 * SUBLANES + rows), value)

    @pl.loop(0, 4)
    def _(k):
        e = jnp.where(k == 0, base, top - 2 + k)
        step_plane(0, shift, first, e, 2, second.put)

    @pl.loop(0, 2)
    def _(k):
        step_plane(0, shift, first, jnp.where(k == 0, base - 1, top + 2), 0, second.put)

    @pl.when(at_top & (shift == 0))
    def _():
        bring_top(second)

    @pl.loop(base + 1, top + 1)
    def _(e):
        step_plane(1, shift, second, e, 1, first.put)

    @pl.loop(0, 2)
    def _(k):
        step_plane(1, shift, second, jnp.where(k == 0, base, top + 1), 0, first.put)

    @pl.when(at_top & (shift == 1))
    def _():
        bring_top(first)

    def out_copy(which, j):
        buf, out = ((phi_buf, phi_out), (sol_buf, sol_out))[which]
        return pltpu.make_async_copy(buf.at[j], out.at[j], sems.at[1 + which * planes + j])

    @pl.loop(0, planes)
    def _(j):
        def finish(e, t, at, p, u):
            place = (j, slice(at.start - SUBLANES, at.stop - SUBLANES), slice(t * LANES, (t + 1) * LANES))
            phi_buf[place] = p
            sol_buf[place] = u

        step_plane(2, shift, first, j + base + 1, 0, finish)
        out_copy(0, j).start()
        out_copy(1, j).start()

    for j in range(planes):
        out_copy(0, j).wait()
        out_copy(1, j).wait()


def early(shift, phi, sol, bulk_a, bulk_b, sol_up, side, cross):
    planes, rows, cols = phi.shape
    state = array(planes + BELOW + ABOVE, cols // LANES + 1, rows + 2 * SUBLANES, LANES)
    return pl.pallas_call(
        functools.partial(early_kernel, planes),
        out_shape=(state,) * 6,
        in_specs=[SMEM, HBM, HBM] + [VMEM] * 5,
        out_specs=(VMEM,) * 6,
        scratch_shapes=[
            pltpu.VMEM(phi.shape, F32),
            pltpu.VMEM(phi.shape, F32),
            pltpu.SemaphoreType.DMA((2,)),
        ],
        cost_estimate=cost(64 * phi.size),
        compiler_params=pltpu.CompilerParams(vmem_limit_bytes=12 << 20),
        name="early",
    )(shift, phi, sol, bulk_a, bulk_b, sol_up, side, cross)


def late(shift, side, cross, rim_a, rim_b, seed, state, shape):
    planes = shape[0]
    kept = tuple(jax.ShapeDtypeStruct(s.shape, s.dtype) for s in state)
    out = pl.pallas_call(
        functools.partial(late_kernel, planes),
        out_shape=(array(*shape), array(*shape)) + kept,
        in_specs=[SMEM] + [VMEM] * 4 + [HBM] + [VMEM] * 6,
        out_specs=(HBM, HBM) + (VMEM,) * 6,
        input_output_aliases={6 + k: 2 + k for k in range(6)},
        scratch_shapes=[
            pltpu.VMEM(seed.shape, jnp.int32),
            pltpu.VMEM(shape, F32),
            pltpu.VMEM(shape, F32),
            pltpu.SemaphoreType.DMA((1 + 2 * planes,)),
        ],
        cost_estimate=cost(3 * 64 * state[0].size),
        compiler_params=pltpu.CompilerParams(vmem_limit_bytes=12 << 20),
        name="late",
    )(shift, side, cross, rim_a, rim_b, seed, *state)
    return out[0], out[1]


def swap_edges(message, axis, keep):
    size = lax.axis_size(axis)
    if size <= 2:
        return lax.ppermute(message, axis, ring(size, 1))
    after = lax.ppermute(message, axis, ring(size, -1))
    before = lax.ppermute(message, axis, ring(size, 1))
    return jnp.where(keep, after, before)


def steps(phi, sol, shift_step, seed):
    planes = phi.shape[0]
    size, lanes = lax.axis_size("grow"), lax.axis_size("side")
    both = ("grow", "side")
    even_down, even_up = two_way(size, lanes, -1), two_way(size, lanes, 1)
    sol_up = lax.ppermute(sol, "grow", chain(size, -1))
    side, cross, bulk_a, bulk_b = pack_edges(phi, sol, seed)
    side = swap_edges(side, "side", lane_of(side.shape) < LANES // 2)
    bulk_a = lax.ppermute(bulk_a, both, even_down)
    cross = pack_rows(planes, cross, side)
    rowid = row_of(cross.shape)
    cross = swap_edges(cross, "cross", (rowid < HALF - 1) | (rowid == HALF))
    bulk_b = lax.ppermute(bulk_b, both, even_up)
    rim_a, rim_b = pack_rims(planes, cross, side)
    rim_a = lax.ppermute(rim_a, both, even_down)
    rim_b = lax.ppermute(rim_b, both, even_up)
    state = early(shift_step, phi, sol, bulk_a, bulk_b, sol_up, side, cross)
    return late(shift_step, side, cross, rim_a, rim_b, seed, state, phi.shape)


def solution(mesh):
    return jax.shard_map(
        steps,
        mesh=mesh,
        in_specs=(
            P(("groups", "grow"), "cross", "side"),
            P(("groups", "grow"), "cross", "side"),
            P("groups"),
            P(("groups", "cross"), "side"),
        ),
        out_specs=(P(("groups", "grow"), "cross", "side"), P(("groups", "grow"), "cross", "side")),
        check_vma=False,
    )
```

```python
import functools

import jax
import jax.numpy as jnp
from jax import lax
from jax.experimental import pallas as pl
from jax.experimental.pallas import tpu as pltpu
from jax.sharding import PartitionSpec as P


ITERS = 3
LANES = 128
SUBLANES = 8

partition = 0.15
coupling = 2.0
diffusion = 2.0
spacing_sq = 0.64
time_step = 0.025
gradient_scale = 1.2
drift_rate = 0.01
seed_levels = 1024.0

BELOW = ITERS - 1
ABOVE = ITERS + 1
RIMMED = ITERS
F32 = jnp.float32


def ring(size, by):
    return [(i, (i + by) % size) for i in range(size)]


def two_way(size, lanes, even_by):
    pairs = []
    for g in range(size):
        for c in range(lanes):
            target = g + (even_by if c % 2 == 0 else -even_by)
            inside = 0 <= target < size
            pairs.append((g * lanes + c, target * lanes + c if inside else g * lanes + (c ^ 1)))
    return pairs


def lane_of(shape):
    return lax.broadcasted_iota(jnp.int32, shape, len(shape) - 1)


def row_of(shape):
    return lax.broadcasted_iota(jnp.int32, shape, len(shape) - 2)


def level(seed):
    return seed.astype(F32) / seed_levels - 1.0


VMEM = pl.BlockSpec(memory_space=pltpu.VMEM)
HBM = pl.BlockSpec(memory_space=pltpu.HBM)
SMEM = pl.BlockSpec(memory_space=pltpu.SMEM)
HALF = SUBLANES // 2
LANE_STEP = 2 * SUBLANES


def cost(count):
    return pl.CostEstimate(flops=count, bytes_accessed=4 * count, transcendentals=0)


def in_hbm(x):
    return pltpu.with_memory_space_constraint(x, pltpu.HBM)


def array(*shape):
    return jax.ShapeDtypeStruct(shape, F32)


def start_all(sems, pairs):
    copies = []
    for k, (source, target) in enumerate(pairs):
        copies.append(pltpu.make_async_copy(source, target, sems.at[k]))
        copies[-1].start()
    return copies


def guest_turns(k):
    return (HALF + k, HALF - k)


def odd_core():
    return lax.axis_index("side") % 2 == 1


def edges_kernel(planes, phi, sol, seed, side, cross, cols, rows, seed_cols, seed_rows, sems):
    depth, width = phi.shape[1:]
    left, right = pl.ds(0, LANES), pl.ds(width - LANES, LANES)
    first, last = pl.ds(0, SUBLANES), pl.ds(depth - SUBLANES, SUBLANES)
    every = slice(None)
    copies = start_all(
        sems,
        [
            (phi.at[:, :, left], cols.at[0]),
            (phi.at[:, :, right], cols.at[1]),
            (sol.at[:, :, left], cols.at[2]),
            (sol.at[:, :, right], cols.at[3]),
            (seed.at[:, left], seed_cols.at[0]),
            (seed.at[:, right], seed_cols.at[1]),
            (phi.at[:, first, :], rows.at[0]),
            (phi.at[:, last, :], rows.at[1]),
            (sol.at[:, first, :], rows.at[2]),
            (sol.at[:, last, :], rows.at[3]),
            (seed.at[first, :], seed_rows.at[0]),
            (seed.at[last, :], seed_rows.at[1]),
        ],
    )
    for copy in copies[:6]:
        copy.wait()
    keep = lane_of((depth, LANES)) < LANES // 2
    for k in range(planes):
        side[k] = jnp.where(keep, cols[0, k], cols[1, k])
        side[planes + k] = jnp.where(keep, cols[2, k], cols[3, k])
    side[2 * planes] = level(jnp.where(keep, seed_cols[0], seed_cols[1]))
    for copy in copies[6:]:
        copy.wait()
    rowid = row_of((SUBLANES, width))
    keep = rowid < HALF

    def edge(field, k):
        return jnp.where(keep, rows[2 * field, k], rows[2 * field + 1, k])

    for field in range(2):
        guest = edge(field, planes - 1)
        for k in range(planes - 1):
            cross[field * (planes - 1) + k] = host(rowid, edge(field, k), guest, k)
    cross[2 * (planes - 1)] = level(jnp.where(keep, seed_rows[0], seed_rows[1]))


def parts_kernel(phi, part_a, part_b, final):
    count = part_a.shape[0]
    planes = phi.shape[0]
    low, high = slice(0, count), slice(planes - count, planes)
    final[...] = phi[ABOVE - 1 : ABOVE]

    @pl.when(jnp.logical_not(odd_core()))
    def _():
        part_a[...] = phi[low]
        part_b[...] = phi[high]

    @pl.when(odd_core())
    def _():
        part_a[...] = phi[high]
        part_b[...] = phi[low]


def pack_parts(phi):
    part = array(ABOVE - 1, *phi.shape[1:])
    return pl.pallas_call(
        parts_kernel,
        out_shape=(part, part, array(1, *phi.shape[1:])),
        in_specs=[VMEM],
        out_specs=(VMEM,) * 3,
        cost_estimate=cost(phi.size),
        compiler_params=pltpu.CompilerParams(vmem_limit_bytes=1 << 20),
        name="pack_parts",
    )(phi)


def host(rowid, tile, guest, k):
    low, high = guest_turns(k)
    if k >= RIMMED:
        return tile
    tile = jnp.where(rowid == HALF - 1, pltpu.roll(guest, low, 0), tile)
    return jnp.where(rowid == HALF, pltpu.roll(guest, high, 0), tile)


def hosted(rowid, tiles):
    guest = None
    for k in range(RIMMED):
        low, high = guest_turns(k)
        part = pltpu.roll(tiles[k], SUBLANES - low, 0)
        guest = part if guest is None else jnp.where(rowid == SUBLANES - 1 - k, part, guest)
        part = pltpu.roll(tiles[k], SUBLANES - high, 0)
        guest = jnp.where(rowid == k, part, guest)
    return guest


def pack_edges(phi, sol, seed):
    planes, rows, cols = phi.shape
    return pl.pallas_call(
        functools.partial(edges_kernel, planes),
        out_shape=(
            array(2 * planes + 1, rows, LANES),
            array(2 * planes - 1, SUBLANES, cols),
        ),
        in_specs=[HBM, HBM, HBM],
        out_specs=(VMEM, VMEM),
        scratch_shapes=[
            pltpu.VMEM((4, planes, rows, LANES), F32),
            pltpu.VMEM((4, planes, SUBLANES, cols), F32),
            pltpu.VMEM((2, rows, LANES), jnp.int32),
            pltpu.VMEM((2, SUBLANES, cols), jnp.int32),
            pltpu.SemaphoreType.DMA((12,)),
        ],
        cost_estimate=cost(phi.size),
        compiler_params=pltpu.CompilerParams(vmem_limit_bytes=4 << 20),
        name="pack_edges",
    )(*(in_hbm(x) for x in (phi, sol, seed)))


def rows_kernel(planes, main, side, out):
    width = main.shape[2]
    out[:, :, :width] = main[...]
    rowid = row_of((SUBLANES, LANES))
    keep = rowid < HALF
    depth = side.shape[1]

    def edge(entry):
        return jnp.where(keep, side[entry, :SUBLANES], side[entry, depth - SUBLANES :])

    for field in range(2):
        guest = edge((field + 1) * planes - 1)
        for k in range(planes - 1):
            tile = host(rowid, edge(field * planes + k), guest, k)
            out[field * (planes - 1) + k, :, width:] = tile
    out[2 * (planes - 1), :, width:] = edge(2 * planes)


def pack_rows(planes, main, side):
    count, _, cols = main.shape
    return pl.pallas_call(
        functools.partial(rows_kernel, planes),
        out_shape=array(count, SUBLANES, cols + LANES),
        in_specs=[VMEM, VMEM],
        out_specs=VMEM,
        cost_estimate=cost(main.size),
        compiler_params=pltpu.CompilerParams(vmem_limit_bytes=2 << 20),
        name="pack_rows",
    )(main, side)


def put_row_tile(out, place, tile):
    tiles = tile.shape[1] // LANES
    for t in range(tiles):
        start = (place * tiles + t) * SUBLANES
        out[start : start + SUBLANES, :] = tile[:, t * LANES : (t + 1) * LANES]


def get_row_tile(ref, place, tiles):
    return [
        ref[(place * tiles + t) * SUBLANES : (place * tiles + t + 1) * SUBLANES, :]
        for t in range(tiles)
    ]


def rims_kernel(planes, cross, side, rim_a, rim_b):
    other = planes - 1
    rowid = row_of(cross.shape[1:])
    lanes = lane_of(side.shape[1:])
    inner = (rowid == HALF - 1) | (rowid == HALF)
    middle = (rowid >= HALF - 2) & (rowid < HALF + 2)
    turn = lambda tile: pltpu.roll(tile, HALF, 0)
    depth = side.shape[1]

    def columns(entries):
        packed = side[entries[0]]
        for k, entry in enumerate(entries[1:], 1):
            moved = pltpu.roll(side[entry], k * LANE_STEP, 1)
            near = (lanes >= k * LANE_STEP - HALF) & (lanes < k * LANE_STEP + HALF)
            packed = jnp.where(near, moved, packed)
        return packed

    def fill(down, up):
        put_row_tile(down, 0, jnp.where(inner, turn(cross[2]), cross[0]))
        put_row_tile(down, 1, jnp.where(inner, turn(cross[other + 2]), cross[other]))
        put_row_tile(down, 2, jnp.where(middle, turn(cross[other + 1]), cross[1]))
        down[down.shape[0] - depth :, :] = columns([0, planes, 1, planes + 1, 2, planes + 2])
        put_row_tile(up, 0, jnp.where(inner, cross[other], turn(cross[0])))
        up[up.shape[0] - depth :, :] = columns([planes - 1, 2 * planes - 1])

    @pl.when(jnp.logical_not(odd_core()))
    def _():
        fill(rim_a, rim_b)

    @pl.when(odd_core())
    def _():
        fill(rim_b, rim_a)


def pack_rims(planes, cross, side):
    rim = array(3 * cross.shape[2] // LANES * SUBLANES + side.shape[1], LANES)
    return pl.pallas_call(
        functools.partial(rims_kernel, planes),
        out_shape=(rim, rim),
        in_specs=[VMEM, VMEM],
        out_specs=(VMEM, VMEM),
        cost_estimate=cost(rim.size),
        compiler_params=pltpu.CompilerParams(vmem_limit_bytes=2 << 20),
        name="pack_rims",
    )(cross, side)


class Either:
    def __init__(self, even, odd):
        self.even, self.odd, self.shape = even, odd, even.shape

    def __getitem__(self, at):
        return jnp.where(odd_core(), self.odd[at], self.even[at])


def mobility(phi):
    return 1.0 - jnp.clip(phi, -1.0, 1.0)


class Field:
    def __init__(self, phi, sol, mob, planes):
        self.phi, self.sol, self.mob = phi, sol, mob
        self.planes = planes
        self.tiles = phi.shape[1]
        self.rows = phi.shape[2] - 2 * SUBLANES
        self.base = BELOW
        self.top = BELOW + planes

    def put(self, e, t, at, p, u):
        self.phi[e, t, at, :] = p
        self.sol[e, t, at, :] = u
        self.mob[e, t, at, :] = mobility(p)

    def put_block(self, e, phi, sol, k, j):
        for t in range(self.tiles - 1):
            lanes = slice(t * LANES, (t + 1) * LANES)
            at = slice(SUBLANES, SUBLANES + self.rows)
            self.put(e, t, at, phi[k, :, lanes], sol[j, :, lanes])

    def put_columns(self, e, p, u):
        self.put(e, self.tiles - 1, slice(SUBLANES, SUBLANES + self.rows), p, u)

    def put_rows(self, e, p, u):
        for t in range(self.tiles):
            for start in (0, SUBLANES + self.rows):
                self.put(e, t, slice(start, start + SUBLANES), p[t], u[t])


def ends(step, shift, field, e):
    grow_index = lax.axis_index("grow")
    at_bottom = grow_index == 0
    at_top = grow_index == lax.axis_size("grow") - 1
    moved = shift < step
    low_end = jnp.where(moved, field.base + 1, field.base)
    high_end = jnp.where(moved, field.top, field.top - 1)
    lower = jnp.where(at_bottom & (e == low_end), e, e - 1)
    upper = jnp.where(at_top & (e == high_end), e, e + 1)
    return lower, upper


def covered(field, halo):
    tiles = range(field.tiles if halo else field.tiles - 1)
    first, rows = SUBLANES - halo, field.rows + 2 * halo
    return [(first + k * SUBLANES, tiles) for k in range(-(-rows // SUBLANES))]


def rimmed(field):
    parts = [(1, range(field.tiles)), (SUBLANES + field.rows - 1, range(field.tiles))]
    return parts + [(start, [field.tiles - 1]) for start, _ in covered(field, 0)]


def step_plane(step, shift, source, e, parts, write):
    lower, upper = ends(step, shift, source, e)
    planes = source.planes
    grid_planes = planes * lax.axis_size("grow")
    height = (lax.axis_index("grow") * planes + e - source.base).astype(F32)
    height = jnp.broadcast_to(height, (SUBLANES, LANES))
    temper = gradient_scale * ((height + 0.5) * (1.0 / grid_planes) - 0.5) - drift_rate * step
    pace = time_step / (1.0 - (1.0 - partition) * temper)
    kappa = 0.25 * diffusion * time_step / spacing_sq
    pull = pace * (1.0 / spacing_sq)
    drive = pace * coupling
    rest = pull * 6.0
    tiles = source.tiles
    lanes = lane_of((SUBLANES, LANES))
    heads = lanes == 0
    tails = lanes == LANES - 1
    for start, outputs in parts:

        def load(ref, t, plane=e, by=0):
            return ref[plane, t, start + by : start + by + SUBLANES, :]

        def after(values, t):
            return pltpu.roll(jnp.where(heads, values[(t + 1) % tiles], values[t]), LANES - 1, 1)

        def before(values, t):
            return pltpu.roll(jnp.where(tails, values[t - 1], values[t]), 1, 1)

        p_all = [load(source.phi, t) for t in range(tiles)]
        u_all = [load(source.sol, t) for t in range(tiles)]
        m_all = [load(source.mob, t) for t in range(tiles)]
        flux = [
            (m_all[t] + after(m_all, t)) * (after(u_all, t) - u_all[t]) for t in range(tiles)
        ]
        for t in outputs:
            p, u, m = p_all[t], u_all[t], m_all[t]
            total = after(p_all, t) + before(p_all, t)
            flow = flux[t] - before(flux, t)
            for where in (dict(by=-1), dict(by=1), dict(plane=lower), dict(plane=upper)):
                total = total + load(source.phi, t, **where)
                other = load(source.sol, t, **where)
                flow = flow + (m + load(source.mob, t, **where)) * (other - u)
            well = 1.0 - p * p
            gain = pull * total + p * (pace * well - rest) - drive * (well * well) * (u + temper)
            weight = partition / kappa + (0.5 * (1.0 - partition) / kappa) * m
            change = flow + (0.5 / kappa + (0.5 * (1.0 - partition) / kappa) * u) * gain
            write(e, t, slice(start, start + SUBLANES), p + gain, u + change / weight)


def early_kernel(planes, shift_ref, phi, sol, side, cross, *rest):
    first = Field(*rest[:3], planes)
    second = Field(*rest[3:6], planes)
    base, top, tiles = first.base, first.top, first.tiles
    rowid = row_of((SUBLANES, LANES))
    cut = lambda t: slice(t * LANES, (t + 1) * LANES)
    other = planes - 1
    for k in range(planes):
        first.put_columns(base + k, side[k], side[planes + k])
        if k < other:
            p = [cross[k, :, cut(t)] for t in range(tiles)]
            u = [cross[other + k, :, cut(t)] for t in range(tiles)]
        else:
            p, u = [
                [
                    hosted(rowid, [cross[f * other + j, :, cut(t)] for j in range(RIMMED)])
                    for t in range(tiles)
                ]
                for f in range(2)
            ]
        first.put_rows(base + k, p, u)
    for k in range(planes):
        first.put_block(base + k, phi, sol, k, k)

    @pl.loop(base + 1, top - 1)
    def _(e):
        step_plane(0, shift_ref[0], first, e, covered(first, 2), second.put)


def levels_of(refs, planes):
    return [Field(*refs[k : k + 3], planes) for k in (0, 3, 6)]


def middle_kernel(planes, shift_ref, phi_a, phi_b, sol_a, sol_b, *rest):
    first, second, third = levels_of(rest[6:], planes)
    shift = shift_ref[0]
    base, top = first.base, first.top
    for k in range(ABOVE - 1):
        first.put_block(top + k, Either(phi_a, phi_b), Either(sol_a, sol_b), k, k)
    for k in range(BELOW):
        j = ABOVE - 1 - BELOW + k
        first.put_block(k, Either(phi_b, phi_a), Either(sol_b, sol_a), j, planes - BELOW + k)

    @pl.loop(0, 2)
    def _(k):
        step_plane(0, shift, first, jnp.where(k == 0, base, top - 1), covered(first, 0), second.put)

    @pl.loop(base + 1, top - 1)
    def _(e):
        step_plane(1, shift, second, e, covered(second, 0), third.put)


def late_kernel(planes, shift_ref, side, cross, rim_a, rim_b, seed, *rest):
    first, second, third = levels_of(rest[11:], planes)
    phi_out, sol_out = rest[9:11]
    levels, sems = rest[20:]
    base, top, tiles, rows = first.base, first.top, first.tiles, first.rows
    shift = shift_ref[0]
    at_top = lax.axis_index("grow") == lax.axis_size("grow") - 1
    fetch = pltpu.make_async_copy(seed, levels, sems.at[0])
    fetch.start()
    turn = lambda group: [pltpu.roll(tile, HALF, 0) for tile in group]
    rim_down, rim_up = Either(rim_a, rim_b), Either(rim_b, rim_a)
    p = get_row_tile(rim_down, 0, tiles)
    u = get_row_tile(rim_down, 1, tiles)
    first.put_rows(top, p, u)
    first.put_rows(top + 2, turn(p), turn(u))
    p = get_row_tile(rim_down, 2, tiles)
    first.put_rows(top + 1, p, turn(p))
    p = get_row_tile(rim_up, 0, tiles)
    first.put_rows(base - 1, p, turn(p))

    def spread(packed, k):
        return pltpu.roll(packed, LANES - k * LANE_STEP, 1) if k else packed

    packed = rim_down[rim_down.shape[0] - rows :, :]
    for k in range(RIMMED):
        first.put_columns(top + k, spread(packed, 2 * k), spread(packed, 2 * k + 1))
    packed = rim_up[rim_up.shape[0] - rows :, :]
    first.put_columns(base - 1, packed, spread(packed, 1))
    fetch.wait()

    def bring_top(field):
        def fill(t, at, value):
            field.put(top, t, at, jnp.full(value.shape, -1.0, F32), value)

        body = slice(SUBLANES, SUBLANES + rows)
        for t in range(tiles - 1):
            fill(t, body, level(levels[:, t * LANES : (t + 1) * LANES]))
        fill(tiles - 1, body, side[2 * planes])
        for t in range(tiles):
            value = cross[2 * (planes - 1), :, t * LANES : (t + 1) * LANES]
            fill(t, slice(0, SUBLANES), value)
            fill(t, slice(SUBLANES + rows, 2 * SUBLANES + rows), value)

    @pl.loop(top, top + 2)
    def _(e):
        step_plane(0, shift, first, e, covered(first, 2), second.put)

    @pl.loop(0, 2)
    def _(k):
        step_plane(0, shift, first, jnp.where(k == 0, base, top - 1), rimmed(first), second.put)

    step_plane(0, shift, first, base - 1, covered(first, 0), second.put)

    @pl.when(at_top & (shift == 0))
    def _():
        bring_top(second)

    @pl.loop(top - 1, top + 1)
    def _(e):
        step_plane(1, shift, second, e, covered(second, 1), third.put)

    @pl.loop(base + 1, top - 1)
    def _(e):
        step_plane(1, shift, second, e, rimmed(second), third.put)

    step_plane(1, shift, second, base, covered(second, 0), third.put)

    @pl.when(at_top & (shift == 1))
    def _():
        bring_top(third)

    @pl.loop(base + 1, top)
    def _(e):
        step_plane(2, shift, third, e, covered(third, 0), into(phi_out, sol_out, base + 1))


def into(phi_out, sol_out, lowest):
    def write(e, t, at, p, u):
        at = slice(at.start - SUBLANES, at.stop - SUBLANES)
        lanes = slice(t * LANES, (t + 1) * LANES)
        phi_out[e - lowest, at, lanes] = p
        sol_out[e - lowest, at, lanes] = u

    return write


def final_kernel(planes, shift_ref, phi_last, sol_a, sol_b, phi_in, sol_in, *rest):
    phi_out, sol_out = rest[9:11]
    first, second, third = levels_of(rest[11:], planes)
    phi_buf, sol_buf, sems = rest[20:]
    shift = shift_ref[0]
    top = first.top
    done = pl.ds(0, planes - 1)
    copies = start_all(
        sems, [(phi_in.at[done], phi_out.at[done]), (sol_in.at[done], sol_out.at[done])]
    )
    edge = top + ABOVE - 1
    first.put_block(edge, phi_last, Either(sol_a, sol_b), 0, ABOVE - 1)
    step_plane(0, shift, first, edge - 1, covered(first, 0), second.put)
    step_plane(1, shift, second, edge - 2, covered(second, 0), third.put)
    step_plane(2, shift, third, edge - 3, covered(third, 0), into(phi_buf, sol_buf, edge - 3))
    copies += start_all(
        sems.at[pl.ds(2, 2)],
        [(phi_buf.at[0], phi_out.at[planes - 1]), (sol_buf.at[0], sol_out.at[planes - 1])],
    )
    for copy in copies:
        copy.wait()


def early(shift, phi, sol, side, cross):
    planes, rows, cols = phi.shape
    state = array(planes + BELOW + ABOVE, cols // LANES + 1, rows + 2 * SUBLANES, LANES)
    return pl.pallas_call(
        functools.partial(early_kernel, planes),
        out_shape=(state,) * 6,
        in_specs=[SMEM] + [VMEM] * 4,
        out_specs=(VMEM,) * 6,
        cost_estimate=cost(64 * phi.size),
        compiler_params=pltpu.CompilerParams(vmem_limit_bytes=8 << 20),
        name="early",
    )(shift, phi, sol, side, cross)


def same(arrays):
    return tuple(array(*a.shape) for a in arrays)


def middle(planes, shift, received, state):
    return pl.pallas_call(
        functools.partial(middle_kernel, planes),
        out_shape=same(state) + same(state[:3]),
        in_specs=[SMEM] + [VMEM] * 10,
        out_specs=(VMEM,) * 9,
        input_output_aliases={5 + k: k for k in range(6)},
        cost_estimate=cost(64 * received[0].size),
        compiler_params=pltpu.CompilerParams(vmem_limit_bytes=8 << 20),
        name="middle",
    )(shift, *received, *state)


def late(shift, side, cross, rim_a, rim_b, seed, state, shape):
    out = pl.pallas_call(
        functools.partial(late_kernel, shape[0]),
        out_shape=(array(*shape), array(*shape)) + same(state),
        in_specs=[SMEM] + [VMEM] * 4 + [HBM] + [VMEM] * 9,
        out_specs=(VMEM,) * 11,
        input_output_aliases={6 + k: 2 + k for k in range(9)},
        scratch_shapes=[pltpu.VMEM(seed.shape, jnp.int32), pltpu.SemaphoreType.DMA((1,))],
        cost_estimate=cost(3 * 64 * state[0].size),
        compiler_params=pltpu.CompilerParams(vmem_limit_bytes=8 << 20),
        name="late",
    )(shift, side, cross, rim_a, rim_b, seed, *state)
    return out[:2], out[2:]


def final(shift, phi_last, sol_a, sol_b, outs, state, shape):
    planes = shape[0]
    out = pl.pallas_call(
        functools.partial(final_kernel, planes),
        out_shape=(array(*shape), array(*shape)) + same(state),
        in_specs=[SMEM] + [VMEM] * 14,
        out_specs=(HBM, HBM) + (VMEM,) * 9,
        input_output_aliases={6 + k: 2 + k for k in range(9)},
        scratch_shapes=[
            pltpu.VMEM((1,) + shape[1:], F32),
            pltpu.VMEM((1,) + shape[1:], F32),
            pltpu.SemaphoreType.DMA((4,)),
        ],
        cost_estimate=cost(64 * phi_last.size),
        compiler_params=pltpu.CompilerParams(vmem_limit_bytes=8 << 20),
        name="final",
    )(shift, phi_last, sol_a, sol_b, *outs, *state)
    return out[0], out[1]


def swap_edges(message, axis, keep):
    size = lax.axis_size(axis)
    if size <= 2:
        return lax.ppermute(message, axis, ring(size, 1))
    after = lax.ppermute(message, axis, ring(size, -1))
    before = lax.ppermute(message, axis, ring(size, 1))
    return jnp.where(keep, after, before)


def steps(phi, sol, shift_step, seed):
    planes = phi.shape[0]
    size, lanes = lax.axis_size("grow"), lax.axis_size("side")
    both = ("grow", "side")
    even_down, even_up = two_way(size, lanes, -1), two_way(size, lanes, 1)
    sol_a = lax.ppermute(sol, both, even_down)
    sol_b = lax.ppermute(sol, both, even_up)
    phi_a, phi_b, phi_last = pack_parts(phi)
    phi_a = lax.ppermute(phi_a, both, even_down)
    phi_b = lax.ppermute(phi_b, both, even_up)
    side, cross = pack_edges(phi, sol, seed)
    side = swap_edges(side, "side", lane_of(side.shape) < LANES // 2)
    cross = pack_rows(planes, cross, side)
    rowid = row_of(cross.shape)
    cross = swap_edges(cross, "cross", (rowid < HALF - 1) | (rowid == HALF))
    rim_a, rim_b = pack_rims(planes, cross, side)
    rim_a = lax.ppermute(rim_a, both, even_down)
    rim_b = lax.ppermute(rim_b, both, even_up)
    phi_last = lax.ppermute(phi_last, "grow", ring(size, -1))
    state = early(shift_step, phi, sol, side, cross)
    state = middle(planes, shift_step, (phi_a, phi_b, sol_a, sol_b), state)
    outs, state = late(shift_step, side, cross, rim_a, rim_b, seed, state, phi.shape)
    return final(shift_step, phi_last, sol_a, sol_b, outs, state, phi.shape)


def solution(mesh):
    return jax.shard_map(
        steps,
        mesh=mesh,
        in_specs=(
            P(("groups", "grow"), "cross", "side"),
            P(("groups", "grow"), "cross", "side"),
            P("groups"),
            P(("groups", "cross"), "side"),
        ),
        out_specs=(P(("groups", "grow"), "cross", "side"), P(("groups", "grow"), "cross", "side")),
        check_vma=False,
    )
```

```python
import functools

import jax
import jax.numpy as jnp
from jax import lax
from jax.experimental import pallas as pl
from jax.experimental.pallas import tpu as pltpu
from jax.sharding import PartitionSpec as P


ITERS = 3
LANES = 128
SUBLANES = 8

partition = 0.15
coupling = 2.0
diffusion = 2.0
spacing_sq = 0.64
time_step = 0.025
gradient_scale = 1.2
drift_rate = 0.01
seed_levels = 1024.0

BELOW = ITERS - 1
ABOVE = ITERS + 1
RIMMED = ITERS
F32 = jnp.float32


def ring(size, by):
    return [(i, (i + by) % size) for i in range(size)]


def two_way(size, lanes, even_by):
    pairs = []
    for g in range(size):
        for c in range(lanes):
            target = g + (even_by if c % 2 == 0 else -even_by)
            inside = 0 <= target < size
            pairs.append((g * lanes + c, target * lanes + c if inside else g * lanes + (c ^ 1)))
    return pairs


def lane_of(shape):
    return lax.broadcasted_iota(jnp.int32, shape, len(shape) - 1)


def row_of(shape):
    return lax.broadcasted_iota(jnp.int32, shape, len(shape) - 2)


def level(seed):
    return seed.astype(F32) / seed_levels - 1.0


VMEM = pl.BlockSpec(memory_space=pltpu.VMEM)
HBM = pl.BlockSpec(memory_space=pltpu.HBM)
SMEM = pl.BlockSpec(memory_space=pltpu.SMEM)
HALF = SUBLANES // 2
LANE_STEP = 2 * SUBLANES


def cost(count):
    return pl.CostEstimate(flops=count, bytes_accessed=4 * count, transcendentals=0)


def in_hbm(x):
    return pltpu.with_memory_space_constraint(x, pltpu.HBM)


def array(*shape):
    return jax.ShapeDtypeStruct(shape, F32)


def start_all(sems, pairs):
    copies = []
    for k, (source, target) in enumerate(pairs):
        copies.append(pltpu.make_async_copy(source, target, sems.at[k]))
        copies[-1].start()
    return copies


def guest_turns(k):
    return (HALF + k, HALF - k)


def odd_core():
    return lax.axis_index("side") % 2 == 1


def edges_kernel(planes, phi_in, sol_in, seed_in, side, cross, part, phi, sol, seed, sems):
    depth, width = phi.shape[1:]
    keep = lane_of((depth, LANES)) < LANES // 2
    copies = start_all(sems, [(phi_in, phi), (sol_in, sol), (seed_in, seed)])
    for copy in copies:
        copy.wait()

    def columns(ref, *at):
        first, last = slice(0, LANES), slice(width - LANES, width)
        return jnp.where(keep, ref[(*at, slice(None), first)], ref[(*at, slice(None), last)])

    for k in range(planes):
        side[k] = columns(phi, k)
        side[planes + k] = columns(sol, k)
    side[2 * planes] = level(columns(seed))
    rowid = row_of((SUBLANES, width))
    upper = rowid < HALF

    def edge(ref, *at):
        first, last = slice(0, SUBLANES), slice(depth - SUBLANES, depth)
        return jnp.where(upper, ref[(*at, first)], ref[(*at, last)])

    for field, ref in enumerate((phi, sol)):
        guest = edge(ref, planes - 1)
        for k in range(planes - 1):
            cross[field * (planes - 1) + k] = host(rowid, edge(ref, k), guest, k)
    cross[2 * (planes - 1)] = level(edge(seed))
    count = part.shape[0]

    @pl.when(jnp.logical_not(odd_core()))
    def _():
        part[...] = sol[planes - count : planes]

    @pl.when(odd_core())
    def _():
        part[...] = sol[0:count]


def parts_kernel(phi, sol, part_a, part_b, tops):
    count = part_a.shape[0]
    planes = phi.shape[0]
    low, high = slice(0, count), slice(planes - count, planes)
    tops[0] = phi[ABOVE - 1]
    tops[1] = sol[ABOVE - 1]

    @pl.when(jnp.logical_not(odd_core()))
    def _():
        part_a[...] = phi[low]
        part_b[...] = phi[high]

    @pl.when(odd_core())
    def _():
        part_a[...] = phi[high]
        part_b[...] = phi[low]


def pack_parts(phi, sol):
    part = array(ABOVE - 1, *phi.shape[1:])
    return pl.pallas_call(
        parts_kernel,
        out_shape=(part, part, array(2, *phi.shape[1:])),
        in_specs=[VMEM, VMEM],
        out_specs=(VMEM,) * 3,
        cost_estimate=cost(phi.size),
        compiler_params=pltpu.CompilerParams(vmem_limit_bytes=1 << 20),
        name="pack_parts",
    )(phi, sol)


def host(rowid, tile, guest, k):
    low, high = guest_turns(k)
    if k >= RIMMED:
        return tile
    tile = jnp.where(rowid == HALF - 1, pltpu.roll(guest, low, 0), tile)
    return jnp.where(rowid == HALF, pltpu.roll(guest, high, 0), tile)


def hosted(rowid, tiles):
    guest = None
    for k in range(RIMMED):
        low, high = guest_turns(k)
        part = pltpu.roll(tiles[k], SUBLANES - low, 0)
        guest = part if guest is None else jnp.where(rowid == SUBLANES - 1 - k, part, guest)
        part = pltpu.roll(tiles[k], SUBLANES - high, 0)
        guest = jnp.where(rowid == k, part, guest)
    return guest


def pack_edges(phi, sol, seed):
    planes, rows, cols = phi.shape
    return pl.pallas_call(
        functools.partial(edges_kernel, planes),
        out_shape=(
            array(2 * planes + 1, rows, LANES),
            array(2 * planes - 1, SUBLANES, cols),
            array(ABOVE - 1, rows, cols),
            array(*phi.shape),
            array(*phi.shape),
        ),
        in_specs=[HBM, HBM, HBM],
        out_specs=(VMEM,) * 5,
        scratch_shapes=[pltpu.VMEM(seed.shape, jnp.int32), pltpu.SemaphoreType.DMA((3,))],
        cost_estimate=cost(phi.size),
        compiler_params=pltpu.CompilerParams(vmem_limit_bytes=4 << 20),
        name="pack_edges",
    )(*(in_hbm(x) for x in (phi, sol, seed)))


def rows_kernel(planes, main, side, out):
    across = main.shape[2] // LANES
    for k in range(main.shape[0]):
        for t in range(across):
            out[k * across + t] = main[k, :, t * LANES : (t + 1) * LANES]
    rowid = row_of((SUBLANES, LANES))
    lanes = lane_of((SUBLANES, LANES))
    keep = rowid < HALF
    depth = side.shape[1]

    def edge(entry):
        return jnp.where(keep, side[entry, :SUBLANES], side[entry, depth - SUBLANES :])

    corners = []
    for field in range(2):
        guest = edge((field + 1) * planes - 1)
        for k in range(planes - 1):
            corners.append(host(rowid, edge(field * planes + k), guest, k))
    corners.append(edge(2 * planes))
    packed = corners[0]
    for k, corner in enumerate(corners[1:], 1):
        near = (lanes >= k * LANE_STEP - HALF) & (lanes < k * LANE_STEP + HALF)
        packed = jnp.where(near, pltpu.roll(corner, k * LANE_STEP, 1), packed)
    out[main.shape[0] * across] = packed


def pack_rows(planes, main, side):
    count, _, cols = main.shape
    return pl.pallas_call(
        functools.partial(rows_kernel, planes),
        out_shape=array(count * (cols // LANES) + 1, SUBLANES, LANES),
        in_specs=[VMEM, VMEM],
        out_specs=VMEM,
        cost_estimate=cost(main.size),
        compiler_params=pltpu.CompilerParams(vmem_limit_bytes=2 << 20),
        name="pack_rows",
    )(main, side)


class Rows:
    def __init__(self, ref, planes):
        self.ref, self.main = ref, (ref.shape[0] - 1) // (2 * planes - 1)

    def tile(self, k, t):
        if t < self.main:
            return self.ref[k * self.main + t]
        corner = self.ref[self.ref.shape[0] - 1]
        return pltpu.roll(corner, LANES - k * LANE_STEP, 1) if k else corner

    def __getitem__(self, k):
        return jnp.concatenate([self.tile(k, t) for t in range(self.main + 1)], axis=1)


RIM_TILES = 3


def put_rims(out, tiles, columns):
    lanes = lane_of((SUBLANES, LANES))
    place, corners = 0, None
    for k, tile in enumerate(tiles):
        for start in range(0, tile.shape[1] - LANES, LANES):
            out[place : place + SUBLANES, :] = tile[:, start : start + LANES]
            place += SUBLANES
        corner = tile[:, tile.shape[1] - LANES :]
        if k:
            near = (lanes >= k * LANE_STEP - HALF) & (lanes < k * LANE_STEP + HALF)
            corner = jnp.where(near, pltpu.roll(corner, k * LANE_STEP, 1), corners)
        corners = corner
    place = RIM_TILES * (tiles[0].shape[1] - LANES) // LANES * SUBLANES
    out[place : place + SUBLANES, :] = corners
    depth = columns.shape[0] // 2
    lanes = lane_of((depth, LANES))
    moved = pltpu.roll(columns[depth:], LANES // 2, 1)
    away = (lanes >= LANES // 2 - SUBLANES) & (lanes < LANES - SUBLANES)
    out[place + SUBLANES :, :] = jnp.where(away, moved, columns[:depth])


def get_row_tile(ref, k, tiles):
    main = tiles - 1
    at = lambda n: slice(n * SUBLANES, (n + 1) * SUBLANES)
    corner = ref[at(RIM_TILES * main), :]
    corner = pltpu.roll(corner, LANES - k * LANE_STEP, 1) if k else corner
    return [ref[at(k * main + t), :] for t in range(main)] + [corner]


def get_columns(ref, k, tiles):
    packed = ref[(RIM_TILES * (tiles - 1) + 1) * SUBLANES :, :]
    low = pltpu.roll(packed, LANES - k * SUBLANES, 1) if k else packed
    high = pltpu.roll(packed, LANES // 2 - k * SUBLANES, 1)
    return jnp.concatenate([low, high], axis=0)


def rims_kernel(planes, cross, side, rim_a, rim_b):
    other = planes - 1
    cross = Rows(cross, planes)
    rowid = row_of((SUBLANES, (cross.main + 1) * LANES))
    lanes = lane_of(side.shape[1:])
    inner = (rowid == HALF - 1) | (rowid == HALF)
    middle = (rowid >= HALF - 2) & (rowid < HALF + 2)
    turn = lambda tile: pltpu.roll(tile, HALF, 0)

    def columns(entries):
        packed = side[entries[0]]
        for k, entry in enumerate(entries[1:], 1):
            moved = pltpu.roll(side[entry], k * SUBLANES, 1)
            near = (lanes >= k * SUBLANES - HALF) & (lanes < k * SUBLANES + HALF)
            packed = jnp.where(near, moved, packed)
        return packed

    def fill(down, up):
        tiles = [
            jnp.where(inner, turn(cross[2]), cross[0]),
            jnp.where(inner, turn(cross[other + 2]), cross[other]),
            jnp.where(middle, turn(cross[other + 1]), cross[1]),
        ]
        put_rims(down, tiles, columns([0, planes, 1, planes + 1, 2, planes + 2]))
        tiles = [jnp.where(inner, cross[other], turn(cross[0]))]
        put_rims(up, tiles, columns([planes - 1, 2 * planes - 1]))

    @pl.when(jnp.logical_not(odd_core()))
    def _():
        fill(rim_a, rim_b)

    @pl.when(odd_core())
    def _():
        fill(rim_b, rim_a)


def pack_rims(planes, cross, side):
    main = (cross.shape[0] - 1) // (2 * planes - 1)
    rim = array((RIM_TILES * main + 1) * SUBLANES + side.shape[1] // 2, LANES)
    return pl.pallas_call(
        functools.partial(rims_kernel, planes),
        out_shape=(rim, rim),
        in_specs=[VMEM, VMEM],
        out_specs=(VMEM, VMEM),
        cost_estimate=cost(rim.size),
        compiler_params=pltpu.CompilerParams(vmem_limit_bytes=2 << 20),
        name="pack_rims",
    )(cross, side)


def mobility(phi):
    return 1.0 - jnp.clip(phi, -1.0, 1.0)


class Either:
    def __init__(self, even, odd, even_skip=0, odd_skip=0):
        self.even, self.odd, self.shape = even, odd, even.shape
        self.skips = (even_skip, odd_skip)

    def __getitem__(self, at):
        if any(self.skips):
            even, odd = ((at[0] + skip, *at[1:]) for skip in self.skips)
        else:
            even = odd = at
        return jnp.where(odd_core(), self.odd[odd], self.even[even])


class Field:
    def __init__(self, phi, sol, mob, planes):
        self.phi, self.sol, self.mob = phi, sol, mob
        self.planes = planes
        self.tiles = phi.shape[1]
        self.rows = phi.shape[2] - 2 * SUBLANES
        self.base = BELOW
        self.top = BELOW + planes

    def put(self, e, t, at, p, u):
        self.phi[e, t, at, :] = p
        self.sol[e, t, at, :] = u
        self.mob[e, t, at, :] = mobility(p)

    def put_block(self, e, phi, sol, k, j):
        for t in range(self.tiles - 1):
            lanes = slice(t * LANES, (t + 1) * LANES)
            at = slice(SUBLANES, SUBLANES + self.rows)
            self.put(e, t, at, phi[k, :, lanes], sol[j, :, lanes])

    def put_columns(self, e, p, u):
        self.put(e, self.tiles - 1, slice(SUBLANES, SUBLANES + self.rows), p, u)

    def put_rows(self, e, p, u):
        for t in range(self.tiles):
            for start in (0, SUBLANES + self.rows):
                self.put(e, t, slice(start, start + SUBLANES), p[t], u[t])


def ends(moved, field, e):
    grow_index = lax.axis_index("grow")
    at_bottom = grow_index == 0
    at_top = grow_index == lax.axis_size("grow") - 1
    low_end = jnp.where(moved, field.base + 1, field.base)
    high_end = jnp.where(moved, field.top, field.top - 1)
    lower = jnp.where(at_bottom & (e == low_end), e, e - 1)
    upper = jnp.where(at_top & (e == high_end), e, e + 1)
    return lower, upper


def covered(field, halo):
    tiles = range(field.tiles if halo else field.tiles - 1)
    parts = [(SUBLANES + start, tiles) for start in range(0, field.rows, SUBLANES)]
    return parts + ([halo_part(field, halo)] if halo else [])


def halo_part(field, halo):
    return (SUBLANES + field.rows, range(field.tiles if halo > 1 else field.tiles - 1))


def rimmed(field, halo):
    last = [field.tiles - 1]
    return [halo_part(field, halo)] + [(start, last) for start, _ in covered(field, 0)]


def step_plane(step, moved, source, e, parts, write):
    lower, upper = ends(moved, source, e)
    planes = source.planes
    grid_planes = planes * lax.axis_size("grow")
    height = (lax.axis_index("grow") * planes + e - source.base).astype(F32)
    height = jnp.broadcast_to(height, (SUBLANES, LANES))
    temper = gradient_scale * ((height + 0.5) * (1.0 / grid_planes) - 0.5) - drift_rate * step
    pace = time_step / (1.0 - (1.0 - partition) * temper)
    kappa = 0.25 * diffusion * time_step / spacing_sq
    pull = pace * (1.0 / spacing_sq)
    drive = pace * coupling
    rest = pull * 6.0
    tiles = source.tiles
    lanes = lane_of((SUBLANES, LANES))
    heads = lanes == 0
    tails = lanes == LANES - 1
    for start, outputs in parts:

        outside = start == SUBLANES + source.rows

        def load(ref, t, plane=e, by=0):
            low = 1 if outside and by > 0 else start + by
            return ref[plane, t, low : low + SUBLANES, :]

        def after(values, t):
            return pltpu.roll(jnp.where(heads, values[(t + 1) % tiles], values[t]), LANES - 1, 1)

        def before(values, t):
            return pltpu.roll(jnp.where(tails, values[t - 1], values[t]), 1, 1)

        p_all = [load(source.phi, t) for t in range(tiles)]
        u_all = [load(source.sol, t) for t in range(tiles)]
        m_all = [load(source.mob, t) for t in range(tiles)]
        p_next = [after(p_all, t) for t in range(tiles)]
        flux = [
            (m_all[t] + mobility(p_next[t])) * (after(u_all, t) - u_all[t]) for t in range(tiles)
        ]
        for t in outputs:
            p, u, m = p_all[t], u_all[t], m_all[t]
            total = p_next[t] + before(p_all, t)
            flow = flux[t] - before(flux, t)
            for where in (dict(by=-1), dict(by=1), dict(plane=lower), dict(plane=upper)):
                total = total + load(source.phi, t, **where)
                other = load(source.sol, t, **where)
                flow = flow + (m + load(source.mob, t, **where)) * (other - u)
            well = 1.0 - p * p
            gain = pull * total + p * (pace * well - rest) - drive * (well * well) * (u + temper)
            weight = partition / kappa + (0.5 * (1.0 - partition) / kappa) * m
            change = flow + (0.5 / kappa + (0.5 * (1.0 - partition) / kappa) * u) * gain
            new_p, new_u = p + gain, u + change / weight
            write(e, t, slice(start, start + SUBLANES), new_p, new_u)
            if outside:
                write(e, t, slice(0, SUBLANES), new_p, new_u)


def early_kernel(planes, phi, sol, side, cross, *rest):
    first = Field(*rest[:3], planes)
    second = Field(*rest[3:6], planes)
    base, top, tiles = first.base, first.top, first.tiles
    rowid = row_of((SUBLANES, LANES))
    cross = Rows(cross, planes)
    other = planes - 1
    for k in range(planes):
        first.put_columns(base + k, side[k], side[planes + k])
        if k < other:
            p = [cross.tile(k, t) for t in range(tiles)]
            u = [cross.tile(other + k, t) for t in range(tiles)]
        else:
            p, u = [
                [
                    hosted(rowid, [cross.tile(f * other + j, t) for j in range(RIMMED)])
                    for t in range(tiles)
                ]
                for f in range(2)
            ]
        first.put_rows(base + k, p, u)
    for k in range(planes):
        first.put_block(base + k, phi, sol, k, k)

    @pl.loop(base + 1, top - 1)
    def _(e):
        step_plane(0, False, first, e, covered(first, 2), second.put)


def levels_of(refs, planes):
    return [Field(*refs[k : k + 3], planes) for k in (0, 3, 6)]


def fetch(source, target, sem):
    copy = pltpu.make_async_copy(source, target, sem)
    copy.start()

    def value():
        copy.wait()
        return target[0]

    return value


FETCHED = [pltpu.SMEM((1,), jnp.int32), pltpu.SemaphoreType.DMA]


def middle_kernel(planes, shift_ref, phi_a, phi_b, sol_a, sol_b, *rest):
    first, second, third = levels_of(rest[6:15], planes)
    fetched = fetch(shift_ref, *rest[15:])
    base, top = first.base, first.top
    for k in range(ABOVE - 1):
        first.put_block(top + k, Either(phi_a, phi_b), Either(sol_a, sol_b), k, k)
    for k in range(BELOW):
        j = ABOVE - 1 - BELOW + k
        sol = Either(sol_b, sol_a, 0, planes - ABOVE + 1)
        first.put_block(k, Either(phi_b, phi_a), sol, j, j)

    @pl.loop(0, 2)
    def _(k):
        step_plane(0, False, first, jnp.where(k == 0, base, top - 1), covered(first, 0), second.put)

    moved = fetched() < 1

    @pl.loop(base + 1, top - 1)
    def _(e):
        step_plane(1, moved, second, e, covered(second, 0), third.put)


def late_kernel(planes, shift_ref, side, cross, rim_a, rim_b, levels, *rest):
    first, second, third = levels_of(rest[11:20], planes)
    phi_out, sol_out = rest[9:11]
    fetched = fetch(shift_ref, *rest[20:])
    base, top, tiles, rows = first.base, first.top, first.tiles, first.rows
    at_top = lax.axis_index("grow") == lax.axis_size("grow") - 1
    turn = lambda group: [pltpu.roll(tile, HALF, 0) for tile in group]
    rim_down, rim_up = Either(rim_a, rim_b), Either(rim_b, rim_a)
    p = get_row_tile(rim_down, 0, tiles)
    u = get_row_tile(rim_down, 1, tiles)
    first.put_rows(top, p, u)
    first.put_rows(top + 2, turn(p), turn(u))
    p = get_row_tile(rim_down, 2, tiles)
    first.put_rows(top + 1, p, turn(p))
    p = get_row_tile(rim_up, 0, tiles)
    first.put_rows(base - 1, p, turn(p))

    for k in range(RIMMED):
        p, u = (get_columns(rim_down, 2 * k + f, tiles) for f in range(2))
        first.put_columns(top + k, p, u)
    first.put_columns(base - 1, get_columns(rim_up, 0, tiles), get_columns(rim_up, 1, tiles))

    def bring_top(field):
        def fill(t, at, value):
            field.put(top, t, at, jnp.full(value.shape, -1.0, F32), value)

        body = slice(SUBLANES, SUBLANES + rows)
        for t in range(tiles - 1):
            fill(t, body, level(levels[:, t * LANES : (t + 1) * LANES]))
        fill(tiles - 1, body, side[2 * planes])
        for t in range(tiles):
            value = Rows(cross, planes).tile(2 * (planes - 1), t)
            fill(t, slice(0, SUBLANES), value)
            fill(t, slice(SUBLANES + rows, 2 * SUBLANES + rows), value)

    @pl.loop(top, top + 2)
    def _(e):
        step_plane(0, False, first, e, covered(first, 2), second.put)

    @pl.loop(0, 2)
    def _(k):
        step_plane(0, False, first, jnp.where(k == 0, base, top - 1), rimmed(first, 2), second.put)

    step_plane(0, False, first, base - 1, covered(first, 0), second.put)
    shift = fetched()
    moved = shift < 1

    @pl.when(at_top & (shift == 0))
    def _():
        bring_top(second)

    @pl.loop(top - 1, top + 1)
    def _(e):
        step_plane(1, moved, second, e, covered(second, 1), third.put)

    @pl.loop(base + 1, top - 1)
    def _(e):
        step_plane(1, moved, second, e, rimmed(second, 1), third.put)

    step_plane(1, moved, second, base, covered(second, 0), third.put)

    @pl.when(at_top & (shift == 1))
    def _():
        bring_top(third)

    @pl.loop(base + 1, top)
    def _(e):
        step_plane(2, True, third, e, covered(third, 0), into(phi_out, sol_out, base + 1))


def into(phi_out, sol_out, lowest):
    def write(e, t, at, p, u):
        at = slice(at.start - SUBLANES, at.stop - SUBLANES)
        lanes = slice(t * LANES, (t + 1) * LANES)
        phi_out[e - lowest, at, lanes] = p
        sol_out[e - lowest, at, lanes] = u

    return write


def final_kernel(planes, tops, sol_a, phi_in, sol_in, *rest):
    phi_out, sol_out = rest[9:11]
    first, second, third = levels_of(rest[11:20], planes)
    phi_buf, sol_buf, sems = rest[20:]
    top = first.top
    done = pl.ds(0, planes - 1)
    copies = start_all(
        sems, [(phi_in.at[done], phi_out.at[done]), (sol_in.at[done], sol_out.at[done])]
    )
    edge = top + ABOVE - 1
    first.put_block(edge, tops, Either(sol_a, tops, ABOVE - 1, 1), 0, 0)
    step_plane(0, False, first, edge - 1, covered(first, 0), second.put)
    step_plane(1, False, second, edge - 2, covered(second, 0), third.put)
    step_plane(2, True, third, edge - 3, covered(third, 0), into(phi_buf, sol_buf, edge - 3))
    copies += start_all(
        sems.at[pl.ds(2, 2)],
        [(phi_buf.at[0], phi_out.at[planes - 1]), (sol_buf.at[0], sol_out.at[planes - 1])],
    )
    for copy in copies:
        copy.wait()


def early(phi, sol, side, cross):
    planes, rows, cols = phi.shape
    state = array(planes + BELOW + ABOVE, cols // LANES + 1, rows + 2 * SUBLANES, LANES)
    return pl.pallas_call(
        functools.partial(early_kernel, planes),
        out_shape=(state,) * 6,
        in_specs=[VMEM] * 4,
        out_specs=(VMEM,) * 6,
        cost_estimate=cost(64 * phi.size),
        compiler_params=pltpu.CompilerParams(vmem_limit_bytes=8 << 20),
        name="early",
    )(phi, sol, side, cross)


def same(arrays):
    return tuple(array(*a.shape) for a in arrays)


def middle(planes, shift, received, state):
    return pl.pallas_call(
        functools.partial(middle_kernel, planes),
        out_shape=same(state) + same(state[:3]),
        in_specs=[HBM] + [VMEM] * 10,
        out_specs=(VMEM,) * 9,
        scratch_shapes=FETCHED,
        input_output_aliases={5 + k: k for k in range(6)},
        cost_estimate=cost(64 * received[0].size),
        compiler_params=pltpu.CompilerParams(vmem_limit_bytes=8 << 20),
        name="middle",
    )(shift, *received, *state)


def late(shift, side, cross, rim_a, rim_b, seed, state, shape):
    out = pl.pallas_call(
        functools.partial(late_kernel, shape[0]),
        out_shape=(array(*shape), array(*shape)) + same(state),
        in_specs=[HBM] + [VMEM] * 14,
        out_specs=(VMEM,) * 11,
        scratch_shapes=FETCHED,
        input_output_aliases={6 + k: 2 + k for k in range(9)},
        cost_estimate=cost(3 * 64 * state[0].size),
        compiler_params=pltpu.CompilerParams(vmem_limit_bytes=8 << 20),
        name="late",
    )(shift, side, cross, rim_a, rim_b, seed, *state)
    return out[:2], out[2:]


def final(tops, sol_a, outs, state, shape):
    planes = shape[0]
    out = pl.pallas_call(
        functools.partial(final_kernel, planes),
        out_shape=(array(*shape), array(*shape)) + same(state),
        in_specs=[VMEM] * 13,
        out_specs=(HBM, HBM) + (VMEM,) * 9,
        input_output_aliases={4 + k: 2 + k for k in range(9)},
        scratch_shapes=[
            pltpu.VMEM((1,) + shape[1:], F32),
            pltpu.VMEM((1,) + shape[1:], F32),
            pltpu.SemaphoreType.DMA((4,)),
        ],
        cost_estimate=cost(64 * tops.size),
        compiler_params=pltpu.CompilerParams(vmem_limit_bytes=8 << 20),
        name="final",
    )(tops, sol_a, *outs, *state)
    return out[0], out[1]


def swap_edges(message, axis, keep):
    size = lax.axis_size(axis)
    if size <= 2:
        return lax.ppermute(message, axis, ring(size, 1))
    after = lax.ppermute(message, axis, ring(size, -1))
    before = lax.ppermute(message, axis, ring(size, 1))
    return jnp.where(keep, after, before)


def steps(phi, sol, shift_step, seed):
    planes = phi.shape[0]
    size, lanes = lax.axis_size("grow"), lax.axis_size("side")
    both = ("grow", "side")
    even_down, even_up = two_way(size, lanes, -1), two_way(size, lanes, 1)
    sol_a = lax.ppermute(sol, both, even_down)
    side, cross, sol_b, phi, sol = pack_edges(phi, sol, seed)
    sol_b = lax.ppermute(sol_b, both, even_up)
    phi_a, phi_b, tops = pack_parts(phi, sol)
    phi_a = lax.ppermute(phi_a, both, even_down)
    phi_b = lax.ppermute(phi_b, both, even_up)
    side = swap_edges(side, "side", lane_of(side.shape) < LANES // 2)
    cross = pack_rows(planes, cross, side)
    rowid = row_of(cross.shape)
    cross = swap_edges(cross, "cross", (rowid < HALF - 1) | (rowid == HALF))
    rim_a, rim_b = pack_rims(planes, cross, side)
    rim_a = lax.ppermute(rim_a, both, even_down)
    rim_b = lax.ppermute(rim_b, both, even_up)
    tops = lax.ppermute(tops, "grow", ring(size, -1))
    state = early(phi, sol, side, cross)
    state = middle(planes, shift_step, (phi_a, phi_b, sol_a, sol_b), state)
    outs, state = late(shift_step, side, cross, rim_a, rim_b, seed, state, phi.shape)
    return final(tops, sol_a, outs, state, phi.shape)


def solution(mesh):
    return jax.shard_map(
        steps,
        mesh=mesh,
        in_specs=(
            P(("groups", "grow"), "cross", "side"),
            P(("groups", "grow"), "cross", "side"),
            P("groups"),
            P(("groups", "cross"), "side"),
        ),
        out_specs=(P(("groups", "grow"), "cross", "side"), P(("groups", "grow"), "cross", "side")),
        check_vma=False,
    )
```

```python
import functools

import jax
import jax.numpy as jnp
from jax import lax
from jax.experimental import pallas as pl
from jax.experimental.pallas import tpu as pltpu
from jax.sharding import PartitionSpec as P


ITERS = 3
LANES = 128
SUBLANES = 8

partition = 0.15
coupling = 2.0
diffusion = 2.0
spacing_sq = 0.64
time_step = 0.025
gradient_scale = 1.2
drift_rate = 0.01
seed_levels = 1024.0

BELOW = ITERS - 1
ABOVE = ITERS + 1
RIMMED = ITERS
F32 = jnp.float32


def ring(size, by):
    return [(i, (i + by) % size) for i in range(size)]


def chain(size, by):
    return [(i, i + by) for i in range(size) if 0 <= i + by < size]


def two_way(size, lanes, even_by):
    pairs = []
    for g in range(size):
        for c in range(lanes):
            target = g + (even_by if c % 2 == 0 else -even_by)
            inside = 0 <= target < size
            pairs.append((g * lanes + c, target * lanes + c if inside else g * lanes + (c ^ 1)))
    return pairs


def lane_of(shape):
    return lax.broadcasted_iota(jnp.int32, shape, len(shape) - 1)


def row_of(shape):
    return lax.broadcasted_iota(jnp.int32, shape, len(shape) - 2)


def level(seed):
    return seed.astype(F32) / seed_levels - 1.0


VMEM = pl.BlockSpec(memory_space=pltpu.VMEM)
HBM = pl.BlockSpec(memory_space=pltpu.HBM)
SMEM = pl.BlockSpec(memory_space=pltpu.SMEM)
HALF = SUBLANES // 2
LANE_STEP = 2 * SUBLANES


def cost(count):
    return pl.CostEstimate(flops=count, bytes_accessed=4 * count, transcendentals=0)


def in_hbm(x):
    return pltpu.with_memory_space_constraint(x, pltpu.HBM)


def array(*shape):
    return jax.ShapeDtypeStruct(shape, F32)


def start_all(sems, pairs):
    copies = []
    for k, (source, target) in enumerate(pairs):
        copies.append(pltpu.make_async_copy(source, target, sems.at[k]))
        copies[-1].start()
    return copies


def guest_turns(k):
    return (HALF + k, HALF - k)


def odd_core():
    return lax.axis_index("side") % 2 == 1


def edges_kernel(planes, phi_in, sol_in, seed_in, side, cross, part, phi, sol, seed, sems):
    depth, width = phi.shape[1:]
    keep = lane_of((depth, LANES)) < LANES // 2
    copies = start_all(sems, [(phi_in, phi), (sol_in, sol), (seed_in, seed)])
    for copy in copies:
        copy.wait()

    def columns(ref, *at):
        first, last = slice(0, LANES), slice(width - LANES, width)
        return jnp.where(keep, ref[(*at, slice(None), first)], ref[(*at, slice(None), last)])

    for k in range(planes):
        side[k] = columns(phi, k)
        side[planes + k] = columns(sol, k)
    side[2 * planes] = level(columns(seed))
    rowid = row_of((SUBLANES, width))
    upper = rowid < HALF

    def edge(ref, *at):
        first, last = slice(0, SUBLANES), slice(depth - SUBLANES, depth)
        return jnp.where(upper, ref[(*at, first)], ref[(*at, last)])

    for field, ref in enumerate((phi, sol)):
        guest = edge(ref, planes - 1)
        for k in range(planes - 1):
            cross[field * (planes - 1) + k] = host(rowid, edge(ref, k), guest, k)
    cross[2 * (planes - 1)] = level(edge(seed))
    count = part.shape[0]

    @pl.when(jnp.logical_not(odd_core()))
    def _():
        part[...] = sol[planes - count : planes]

    @pl.when(odd_core())
    def _():
        part[...] = sol[0:count]


def parts_kernel(phi, sol, part_a, part_b, tops):
    count = part_a.shape[0]
    planes = phi.shape[0]
    low, high = slice(0, count), slice(planes - count, planes)
    tops[0] = phi[ABOVE - 1]
    tops[1] = sol[ABOVE - 1]

    @pl.when(jnp.logical_not(odd_core()))
    def _():
        part_a[...] = phi[low]
        part_b[...] = phi[high]

    @pl.when(odd_core())
    def _():
        part_a[...] = phi[high]
        part_b[...] = phi[low]


def pack_parts(phi, sol):
    part = array(ABOVE - 1, *phi.shape[1:])
    return pl.pallas_call(
        parts_kernel,
        out_shape=(part, part, array(2, *phi.shape[1:])),
        in_specs=[VMEM, VMEM],
        out_specs=(VMEM,) * 3,
        cost_estimate=cost(phi.size),
        compiler_params=pltpu.CompilerParams(vmem_limit_bytes=1 << 20),
        name="pack_parts",
    )(phi, sol)


def host(rowid, tile, guest, k):
    low, high = guest_turns(k)
    if k >= RIMMED:
        return tile
    tile = jnp.where(rowid == HALF - 1, pltpu.roll(guest, low, 0), tile)
    return jnp.where(rowid == HALF, pltpu.roll(guest, high, 0), tile)


def hosted(rowid, tiles):
    guest = None
    for k in range(RIMMED):
        low, high = guest_turns(k)
        part = pltpu.roll(tiles[k], SUBLANES - low, 0)
        guest = part if guest is None else jnp.where(rowid == SUBLANES - 1 - k, part, guest)
        part = pltpu.roll(tiles[k], SUBLANES - high, 0)
        guest = jnp.where(rowid == k, part, guest)
    return guest


def pack_edges(phi, sol, seed):
    planes, rows, cols = phi.shape
    return pl.pallas_call(
        functools.partial(edges_kernel, planes),
        out_shape=(
            array(2 * planes + 1, rows, LANES),
            array(2 * planes - 1, SUBLANES, cols),
            array(ABOVE - 1, rows, cols),
            array(*phi.shape),
            array(*phi.shape),
        ),
        in_specs=[HBM, HBM, HBM],
        out_specs=(VMEM,) * 5,
        scratch_shapes=[pltpu.VMEM(seed.shape, jnp.int32), pltpu.SemaphoreType.DMA((3,))],
        cost_estimate=cost(phi.size),
        compiler_params=pltpu.CompilerParams(vmem_limit_bytes=4 << 20),
        name="pack_edges",
    )(*(in_hbm(x) for x in (phi, sol, seed)))


def rows_kernel(planes, main, side, out):
    across = main.shape[2] // LANES
    for k in range(main.shape[0]):
        for t in range(across):
            out[k * across + t] = main[k, :, t * LANES : (t + 1) * LANES]
    rowid = row_of((SUBLANES, LANES))
    lanes = lane_of((SUBLANES, LANES))
    keep = rowid < HALF
    depth = side.shape[1]

    def edge(entry):
        return jnp.where(keep, side[entry, :SUBLANES], side[entry, depth - SUBLANES :])

    corners = []
    for field in range(2):
        guest = edge((field + 1) * planes - 1)
        for k in range(planes - 1):
            corners.append(host(rowid, edge(field * planes + k), guest, k))
    corners.append(edge(2 * planes))
    packed = corners[0]
    for k, corner in enumerate(corners[1:], 1):
        near = (lanes >= k * LANE_STEP - HALF) & (lanes < k * LANE_STEP + HALF)
        packed = jnp.where(near, pltpu.roll(corner, k * LANE_STEP, 1), packed)
    out[main.shape[0] * across] = packed


def pack_rows(planes, main, side):
    count, _, cols = main.shape
    return pl.pallas_call(
        functools.partial(rows_kernel, planes),
        out_shape=array(count * (cols // LANES) + 1, SUBLANES, LANES),
        in_specs=[VMEM, VMEM],
        out_specs=VMEM,
        cost_estimate=cost(main.size),
        compiler_params=pltpu.CompilerParams(vmem_limit_bytes=2 << 20),
        name="pack_rows",
    )(main, side)


class Rows:
    def __init__(self, ref, planes):
        self.ref, self.main = ref, (ref.shape[0] - 1) // (2 * planes - 1)

    def tile(self, k, t):
        if t < self.main:
            return self.ref[k * self.main + t]
        corner = self.ref[self.ref.shape[0] - 1]
        return pltpu.roll(corner, LANES - k * LANE_STEP, 1) if k else corner

    def __getitem__(self, k):
        return jnp.concatenate([self.tile(k, t) for t in range(self.main + 1)], axis=1)


RIM_TILES = 3


def put_rims(out, tiles, columns):
    lanes = lane_of((SUBLANES, LANES))
    place, corners = 0, None
    for k, tile in enumerate(tiles):
        for start in range(0, tile.shape[1] - LANES, LANES):
            out[place : place + SUBLANES, :] = tile[:, start : start + LANES]
            place += SUBLANES
        corner = tile[:, tile.shape[1] - LANES :]
        if k:
            near = (lanes >= k * LANE_STEP - HALF) & (lanes < k * LANE_STEP + HALF)
            corner = jnp.where(near, pltpu.roll(corner, k * LANE_STEP, 1), corners)
        corners = corner
    place = RIM_TILES * (tiles[0].shape[1] - LANES) // LANES * SUBLANES
    out[place : place + SUBLANES, :] = corners
    depth = columns.shape[0] // 2
    lanes = lane_of((depth, LANES))
    moved = pltpu.roll(columns[depth:], LANES // 2, 1)
    away = (lanes >= LANES // 2 - SUBLANES) & (lanes < LANES - SUBLANES)
    out[place + SUBLANES :, :] = jnp.where(away, moved, columns[:depth])


def get_row_tile(ref, k, tiles):
    main = tiles - 1
    at = lambda n: slice(n * SUBLANES, (n + 1) * SUBLANES)
    corner = ref[at(RIM_TILES * main), :]
    corner = pltpu.roll(corner, LANES - k * LANE_STEP, 1) if k else corner
    return [ref[at(k * main + t), :] for t in range(main)] + [corner]


def get_columns(ref, k, tiles):
    packed = ref[(RIM_TILES * (tiles - 1) + 1) * SUBLANES :, :]
    low = pltpu.roll(packed, LANES - k * SUBLANES, 1) if k else packed
    high = pltpu.roll(packed, LANES // 2 - k * SUBLANES, 1)
    return jnp.concatenate([low, high], axis=0)


def rims_kernel(planes, cross, side, rim_a, rim_b):
    other = planes - 1
    cross = Rows(cross, planes)
    rowid = row_of((SUBLANES, (cross.main + 1) * LANES))
    lanes = lane_of(side.shape[1:])
    inner = (rowid == HALF - 1) | (rowid == HALF)
    middle = (rowid >= HALF - 2) & (rowid < HALF + 2)
    turn = lambda tile: pltpu.roll(tile, HALF, 0)

    def columns(entries):
        packed = side[entries[0]]
        for k, entry in enumerate(entries[1:], 1):
            moved = pltpu.roll(side[entry], k * SUBLANES, 1)
            near = (lanes >= k * SUBLANES - HALF) & (lanes < k * SUBLANES + HALF)
            packed = jnp.where(near, moved, packed)
        return packed

    def fill(down, up):
        tiles = [
            jnp.where(inner, turn(cross[2]), cross[0]),
            jnp.where(inner, turn(cross[other + 2]), cross[other]),
            jnp.where(middle, turn(cross[other + 1]), cross[1]),
        ]
        put_rims(down, tiles, columns([0, planes, 1, planes + 1, 2, planes + 2]))
        tiles = [jnp.where(inner, cross[other], turn(cross[0]))]
        put_rims(up, tiles, columns([planes - 1, 2 * planes - 1]))

    @pl.when(jnp.logical_not(odd_core()))
    def _():
        fill(rim_a, rim_b)

    @pl.when(odd_core())
    def _():
        fill(rim_b, rim_a)


def pack_rims(planes, cross, side):
    main = (cross.shape[0] - 1) // (2 * planes - 1)
    rim = array((RIM_TILES * main + 1) * SUBLANES + side.shape[1] // 2, LANES)
    return pl.pallas_call(
        functools.partial(rims_kernel, planes),
        out_shape=(rim, rim),
        in_specs=[VMEM, VMEM],
        out_specs=(VMEM, VMEM),
        cost_estimate=cost(rim.size),
        compiler_params=pltpu.CompilerParams(vmem_limit_bytes=2 << 20),
        name="pack_rims",
    )(cross, side)


def mobility(phi):
    return 1.0 - jnp.clip(phi, -1.0, 1.0)


def carry_kernel(shift_ref, out):
    out[...] = jnp.full(out.shape, shift_ref[0], jnp.int32)


def carry(shift):
    return pl.pallas_call(
        carry_kernel,
        out_shape=jax.ShapeDtypeStruct((SUBLANES, LANES), jnp.int32),
        in_specs=[SMEM],
        out_specs=VMEM,
        cost_estimate=cost(SUBLANES * LANES),
        compiler_params=pltpu.CompilerParams(vmem_limit_bytes=1 << 20),
        name="carry",
    )(shift)


class Either:
    def __init__(self, even, odd, even_skip=0, odd_skip=0):
        self.even, self.odd, self.shape = even, odd, even.shape
        self.skips = (even_skip, odd_skip)

    def __getitem__(self, at):
        if any(self.skips):
            even, odd = ((at[0] + skip, *at[1:]) for skip in self.skips)
        else:
            even = odd = at
        return jnp.where(odd_core(), self.odd[odd], self.even[even])


class Field:
    def __init__(self, phi, sol, mob, planes):
        self.phi, self.sol, self.mob = phi, sol, mob
        self.planes = planes
        self.tiles = phi.shape[1]
        self.rows = phi.shape[2] - 2 * SUBLANES
        self.base = BELOW
        self.top = BELOW + planes

    def put(self, e, t, at, p, u):
        self.phi[e, t, at, :] = p
        self.sol[e, t, at, :] = u
        self.mob[e, t, at, :] = mobility(p)

    def put_block(self, e, phi, sol, k, j):
        for t in range(self.tiles - 1):
            lanes = slice(t * LANES, (t + 1) * LANES)
            at = slice(SUBLANES, SUBLANES + self.rows)
            self.put(e, t, at, phi[k, :, lanes], sol[j, :, lanes])

    def put_columns(self, e, p, u):
        self.put(e, self.tiles - 1, slice(SUBLANES, SUBLANES + self.rows), p, u)

    def put_rows(self, e, p, u):
        for t in range(self.tiles):
            for start in (0, SUBLANES + self.rows):
                self.put(e, t, slice(start, start + SUBLANES), p[t], u[t])


def ends(moved, field, e):
    grow_index = lax.axis_index("grow")
    at_bottom = grow_index == 0
    at_top = grow_index == lax.axis_size("grow") - 1
    low_end = jnp.where(moved, field.base + 1, field.base)
    high_end = jnp.where(moved, field.top, field.top - 1)
    lower = jnp.where(at_bottom & (e == low_end), e, e - 1)
    upper = jnp.where(at_top & (e == high_end), e, e + 1)
    return lower, upper


def covered(field, halo):
    tiles = range(field.tiles if halo else field.tiles - 1)
    parts = [(SUBLANES + start, tiles) for start in range(0, field.rows, SUBLANES)]
    return parts + ([halo_part(field, halo)] if halo else [])


def halo_part(field, halo):
    return (SUBLANES + field.rows, range(field.tiles if halo > 1 else field.tiles - 1))


def rimmed(field, halo):
    last = [field.tiles - 1]
    return [halo_part(field, halo)] + [(start, last) for start, _ in covered(field, 0)]


def step_plane(step, moved, source, e, parts, write):
    lower, upper = ends(moved, source, e)
    planes = source.planes
    grid_planes = planes * lax.axis_size("grow")
    height = (lax.axis_index("grow") * planes + e - source.base).astype(F32)
    height = jnp.broadcast_to(height, (SUBLANES, LANES))
    temper = gradient_scale * ((height + 0.5) * (1.0 / grid_planes) - 0.5) - drift_rate * step
    pace = time_step / (1.0 - (1.0 - partition) * temper)
    kappa = 0.25 * diffusion * time_step / spacing_sq
    pull = pace * (1.0 / spacing_sq)
    drive = pace * coupling
    rest = pull * 6.0
    tiles = source.tiles
    lanes = lane_of((SUBLANES, LANES))
    heads = lanes == 0
    tails = lanes == LANES - 1
    for start, outputs in parts:

        outside = start == SUBLANES + source.rows

        def load(ref, t, plane=e, by=0):
            low = 1 if outside and by > 0 else start + by
            return ref[plane, t, low : low + SUBLANES, :]

        def after(values, t):
            return pltpu.roll(jnp.where(heads, values[(t + 1) % tiles], values[t]), LANES - 1, 1)

        def before(values, t):
            return pltpu.roll(jnp.where(tails, values[t - 1], values[t]), 1, 1)

        p_all = [load(source.phi, t) for t in range(tiles)]
        u_all = [load(source.sol, t) for t in range(tiles)]
        m_all = [load(source.mob, t) for t in range(tiles)]
        p_next = [after(p_all, t) for t in range(tiles)]
        flux = [
            (m_all[t] + mobility(p_next[t])) * (after(u_all, t) - u_all[t]) for t in range(tiles)
        ]
        for t in outputs:
            p, u, m = p_all[t], u_all[t], m_all[t]
            total = p_next[t] + before(p_all, t)
            flow = flux[t] - before(flux, t)
            for where in (dict(by=-1), dict(by=1), dict(plane=lower), dict(plane=upper)):
                total = total + load(source.phi, t, **where)
                other = load(source.sol, t, **where)
                flow = flow + (m + load(source.mob, t, **where)) * (other - u)
            well = 1.0 - p * p
            gain = pull * total + p * (pace * well - rest) - drive * (well * well) * (u + temper)
            weight = partition / kappa + (0.5 * (1.0 - partition) / kappa) * m
            change = flow + (0.5 / kappa + (0.5 * (1.0 - partition) / kappa) * u) * gain
            new_p, new_u = p + gain, u + change / weight
            write(e, t, slice(start, start + SUBLANES), new_p, new_u)
            if outside:
                write(e, t, slice(0, SUBLANES), new_p, new_u)


def early_kernel(planes, phi, sol, side, cross, *rest):
    first = Field(*rest[:3], planes)
    second = Field(*rest[3:6], planes)
    base, top, tiles = first.base, first.top, first.tiles
    rowid = row_of((SUBLANES, LANES))
    cross = Rows(cross, planes)
    other = planes - 1
    for k in range(planes):
        first.put_columns(base + k, side[k], side[planes + k])
        if k < other:
            p = [cross.tile(k, t) for t in range(tiles)]
            u = [cross.tile(other + k, t) for t in range(tiles)]
        else:
            p, u = [
                [
                    hosted(rowid, [cross.tile(f * other + j, t) for j in range(RIMMED)])
                    for t in range(tiles)
                ]
                for f in range(2)
            ]
        first.put_rows(base + k, p, u)
    for k in range(planes):
        first.put_block(base + k, phi, sol, k, k)

    @pl.loop(base + 1, top - 1)
    def _(e):
        step_plane(0, False, first, e, covered(first, 2), second.put)


def levels_of(refs, planes):
    return [Field(*refs[k : k + 3], planes) for k in (0, 3, 6)]


def fetch(source, target, sem):
    copy = pltpu.make_async_copy(source, target, sem)
    copy.start()

    def value():
        copy.wait()
        return target[0, 0]

    return value


FETCHED = [pltpu.SMEM((SUBLANES, LANES), jnp.int32), pltpu.SemaphoreType.DMA]


def middle_kernel(planes, shift_ref, phi_a, phi_b, sol_a, sol_b, *rest):
    first, second, third = levels_of(rest[6:15], planes)
    fetched = fetch(shift_ref, *rest[15:])
    base, top = first.base, first.top
    for k in range(ABOVE - 1):
        first.put_block(top + k, Either(phi_a, phi_b), Either(sol_a, sol_b), k, k)
    for k in range(BELOW):
        j = ABOVE - 1 - BELOW + k
        sol = Either(sol_b, sol_a, 0, planes - ABOVE + 1)
        first.put_block(k, Either(phi_b, phi_a), sol, j, j)

    @pl.loop(0, 2)
    def _(k):
        step_plane(0, False, first, jnp.where(k == 0, base, top - 1), covered(first, 0), second.put)

    moved = fetched() < 1

    @pl.loop(base + 1, top - 1)
    def _(e):
        step_plane(1, moved, second, e, covered(second, 0), third.put)


def late_kernel(planes, shift_ref, side, cross, rim_a, rim_b, levels, *rest):
    first, second, third = levels_of(rest[11:20], planes)
    phi_out, sol_out = rest[9:11]
    fetched = fetch(shift_ref, *rest[20:])
    base, top, tiles, rows = first.base, first.top, first.tiles, first.rows
    at_top = lax.axis_index("grow") == lax.axis_size("grow") - 1
    turn = lambda group: [pltpu.roll(tile, HALF, 0) for tile in group]
    rim_down, rim_up = Either(rim_a, rim_b), Either(rim_b, rim_a)
    p = get_row_tile(rim_down, 0, tiles)
    u = get_row_tile(rim_down, 1, tiles)
    first.put_rows(top, p, u)
    first.put_rows(top + 2, turn(p), turn(u))
    p = get_row_tile(rim_down, 2, tiles)
    first.put_rows(top + 1, p, turn(p))
    p = get_row_tile(rim_up, 0, tiles)
    first.put_rows(base - 1, p, turn(p))

    for k in range(RIMMED):
        p, u = (get_columns(rim_down, 2 * k + f, tiles) for f in range(2))
        first.put_columns(top + k, p, u)
    first.put_columns(base - 1, get_columns(rim_up, 0, tiles), get_columns(rim_up, 1, tiles))

    def bring_top(field):
        def fill(t, at, value):
            field.put(top, t, at, jnp.full(value.shape, -1.0, F32), value)

        body = slice(SUBLANES, SUBLANES + rows)
        for t in range(tiles - 1):
            fill(t, body, level(levels[:, t * LANES : (t + 1) * LANES]))
        fill(tiles - 1, body, side[2 * planes])
        for t in range(tiles):
            value = Rows(cross, planes).tile(2 * (planes - 1), t)
            fill(t, slice(0, SUBLANES), value)
            fill(t, slice(SUBLANES + rows, 2 * SUBLANES + rows), value)

    @pl.loop(top, top + 2)
    def _(e):
        step_plane(0, False, first, e, covered(first, 2), second.put)

    @pl.loop(0, 2)
    def _(k):
        step_plane(0, False, first, jnp.where(k == 0, base, top - 1), rimmed(first, 2), second.put)

    step_plane(0, False, first, base - 1, covered(first, 0), second.put)
    shift = fetched()
    moved = shift < 1

    @pl.when(at_top & (shift == 0))
    def _():
        bring_top(second)

    @pl.loop(top - 1, top + 1)
    def _(e):
        step_plane(1, moved, second, e, covered(second, 1), third.put)

    @pl.loop(base + 1, top - 1)
    def _(e):
        step_plane(1, moved, second, e, rimmed(second, 1), third.put)

    step_plane(1, moved, second, base, covered(second, 0), third.put)

    @pl.when(at_top & (shift == 1))
    def _():
        bring_top(third)

    @pl.loop(base + 1, top)
    def _(e):
        step_plane(2, True, third, e, covered(third, 0), into(phi_out, sol_out, base + 1))


def into(phi_out, sol_out, lowest):
    def write(e, t, at, p, u):
        at = slice(at.start - SUBLANES, at.stop - SUBLANES)
        lanes = slice(t * LANES, (t + 1) * LANES)
        phi_out[e - lowest, at, lanes] = p
        sol_out[e - lowest, at, lanes] = u

    return write


def final_kernel(planes, tops, sol_a, phi_in, sol_in, *rest):
    phi_out, sol_out = rest[9:11]
    first, second, third = levels_of(rest[11:20], planes)
    phi_buf, sol_buf, sems = rest[20:]
    top = first.top
    done = pl.ds(0, planes - 1)
    copies = start_all(
        sems, [(phi_in.at[done], phi_out.at[done]), (sol_in.at[done], sol_out.at[done])]
    )
    edge = top + ABOVE - 1
    first.put_block(edge, tops, Either(sol_a, tops, ABOVE - 1, 1), 0, 0)
    step_plane(0, False, first, edge - 1, covered(first, 0), second.put)
    step_plane(1, False, second, edge - 2, covered(second, 0), third.put)
    step_plane(2, True, third, edge - 3, covered(third, 0), into(phi_buf, sol_buf, edge - 3))
    copies += start_all(
        sems.at[pl.ds(2, 2)],
        [(phi_buf.at[0], phi_out.at[planes - 1]), (sol_buf.at[0], sol_out.at[planes - 1])],
    )
    for copy in copies:
        copy.wait()


def early(phi, sol, side, cross):
    planes, rows, cols = phi.shape
    state = array(planes + BELOW + ABOVE, cols // LANES + 1, rows + 2 * SUBLANES, LANES)
    return pl.pallas_call(
        functools.partial(early_kernel, planes),
        out_shape=(state,) * 6,
        in_specs=[VMEM] * 4,
        out_specs=(VMEM,) * 6,
        cost_estimate=cost(64 * phi.size),
        compiler_params=pltpu.CompilerParams(vmem_limit_bytes=8 << 20),
        name="early",
    )(phi, sol, side, cross)


def same(arrays):
    return tuple(array(*a.shape) for a in arrays)


def middle(planes, shift, received, state):
    return pl.pallas_call(
        functools.partial(middle_kernel, planes),
        out_shape=same(state) + same(state[:3]),
        in_specs=[VMEM] * 11,
        out_specs=(VMEM,) * 9,
        scratch_shapes=FETCHED,
        input_output_aliases={5 + k: k for k in range(6)},
        cost_estimate=cost(64 * received[0].size),
        compiler_params=pltpu.CompilerParams(vmem_limit_bytes=8 << 20),
        name="middle",
    )(shift, *received, *state)


def late(shift, side, cross, rim_a, rim_b, seed, state, shape):
    out = pl.pallas_call(
        functools.partial(late_kernel, shape[0]),
        out_shape=(array(*shape), array(*shape)) + same(state),
        in_specs=[VMEM] * 15,
        out_specs=(VMEM,) * 11,
        scratch_shapes=FETCHED,
        input_output_aliases={6 + k: 2 + k for k in range(9)},
        cost_estimate=cost(3 * 64 * state[0].size),
        compiler_params=pltpu.CompilerParams(vmem_limit_bytes=8 << 20),
        name="late",
    )(shift, side, cross, rim_a, rim_b, seed, *state)
    return out[:2], out[2:]


def final(tops, sol_a, outs, state, shape):
    planes = shape[0]
    out = pl.pallas_call(
        functools.partial(final_kernel, planes),
        out_shape=(array(*shape), array(*shape)) + same(state),
        in_specs=[VMEM] * 13,
        out_specs=(HBM, HBM) + (VMEM,) * 9,
        input_output_aliases={4 + k: 2 + k for k in range(9)},
        scratch_shapes=[
            pltpu.VMEM((1,) + shape[1:], F32),
            pltpu.VMEM((1,) + shape[1:], F32),
            pltpu.SemaphoreType.DMA((4,)),
        ],
        cost_estimate=cost(64 * tops.size),
        compiler_params=pltpu.CompilerParams(vmem_limit_bytes=8 << 20),
        name="final",
    )(tops, sol_a, *outs, *state)
    return out[0], out[1]


def swap_edges(message, axis, keep):
    size = lax.axis_size(axis)
    if size <= 2:
        return lax.ppermute(message, axis, ring(size, 1))
    after = lax.ppermute(message, axis, ring(size, -1))
    before = lax.ppermute(message, axis, ring(size, 1))
    return jnp.where(keep, after, before)


def steps(phi, sol, shift_step, seed):
    planes = phi.shape[0]
    size, lanes = lax.axis_size("grow"), lax.axis_size("side")
    both = ("grow", "side")
    even_down, even_up = two_way(size, lanes, -1), two_way(size, lanes, 1)
    sol_a = lax.ppermute(sol, both, even_down)
    side, cross, sol_b, phi, sol = pack_edges(phi, sol, seed)
    sol_b = lax.ppermute(sol_b, both, even_up)
    phi_a, phi_b, tops = pack_parts(phi, sol)
    phi_a = lax.ppermute(phi_a, both, even_down)
    phi_b = lax.ppermute(phi_b, both, even_up)
    side = swap_edges(side, "side", lane_of(side.shape) < LANES // 2)
    cross = pack_rows(planes, cross, side)
    rowid = row_of(cross.shape)
    cross = swap_edges(cross, "cross", (rowid < HALF - 1) | (rowid == HALF))
    shift_step = carry(shift_step)
    rim_a, rim_b = pack_rims(planes, cross, side)
    rim_a = lax.ppermute(rim_a, both, even_down)
    rim_b = lax.ppermute(rim_b, both, even_up)
    tops = lax.ppermute(tops, "grow", chain(size, -1))
    state = early(phi, sol, side, cross)
    state = middle(planes, shift_step, (phi_a, phi_b, sol_a, sol_b), state)
    outs, state = late(shift_step, side, cross, rim_a, rim_b, seed, state, phi.shape)
    return final(tops, sol_a, outs, state, phi.shape)


def solution(mesh):
    return jax.shard_map(
        steps,
        mesh=mesh,
        in_specs=(
            P(("groups", "grow"), "cross", "side"),
            P(("groups", "grow"), "cross", "side"),
            P("groups"),
            P(("groups", "cross"), "side"),
        ),
        out_specs=(P(("groups", "grow"), "cross", "side"), P(("groups", "grow"), "cross", "side")),
        check_vma=False,
    )
```
